32 devices in a mesh: echo: 2 (over x), coil: 8 (over z, core), read: 2 (over y).
Axes of the slice: x: 2, y: 2, z: 4, core: 2. Of those that a mesh axis runs over, the one named last changes fastest.
Arguments:
- kspace: bfloat16 [384, 2, 8, 4, 2, 192], P(None, 'echo', 'coil', 'read'), may hold values from -3 to 3
- sampling: int32 [384, 2, 192], P(None, 'echo'), may hold values 0 or 1
- coil_maps: bfloat16 [384, 8, 4, 2, 192], P(None, 'coil', 'read'), may hold values from -1.5 to 1.5
- image: float32 [384, 2, 4, 2, 192], P('coil', 'echo', 'read'), may hold values from -6 to 6
- filters: bfloat16 [48, 3, 3, 3, 2], replicated, may hold values from -0.875 to 0.875
- thresholds: float32 [48], replicated, may hold values from 0.5 to 8
- dc_weight: float32 [2], P('echo'), may hold values from 0.5 to 2
Outputs:
- updated: float32 [384, 2, 4, 2, 192], P('coil', 'echo', 'read')
The draws below stay inside these ranges and needn't reach their ends.
All inputs are finite; a program needn't handle non-finite values. No bound on the sum of `sampling` on one device may be relied on, other than what follows from the above.
Results may differ from the reference program's by a relative error of at most 0.0033.
Values may be sent and summed in bfloat16 or wider, within the bound.
A program may use at most 128 MiB of HBM per device.

```python
import math
import jax
import jax.numpy as jnp
from jax import lax

NY = 384
NZ = 192
FILTERS = 48
ECHOES = 2
COILS = 8
RO = 4


def plant(values, rng, low, high):
    extent = values.shape
    index_at = [jax.random.randint(jax.random.fold_in(rng, axis), (), 0, extent[axis]) for axis in range(len(extent))]
    values = values.at[tuple(index_at)].set(low)
    longest = extent.index(max(extent))
    index_at[longest] = (index_at[longest] + 1) % extent[longest]
    return values.at[tuple(index_at)].set(high)


def shard_levels(rng, dims, shards, smallest, largest):
    def one(axis_at, shards_of):
        steps = jax.random.uniform(jax.random.fold_in(jax.random.fold_in(rng, 6), axis_at), (shards_of,), jnp.float32, smallest / len(shards), largest / len(shards))
        return jnp.repeat(jnp.exp(steps), dims[axis_at] // shards_of).reshape((-1,) + (1,) * (len(dims) - axis_at - 1))

    factor_of = one(*shards[0])
    for cut in shards[1:]:
        factor_of = factor_of * one(*cut)
    return factor_of


def noise(key, dims, scale, reach, cuts=(), held_as=jnp.bfloat16):
    drawn = scale * jax.random.normal(key, dims, jnp.float32)
    if cuts:
        drawn = drawn * shard_levels(key, dims, cuts, -0.22, 0.18)
    return jnp.clip(drawn, -reach, reach).astype(held_as)


def setup_inputs(seed: int = 0) -> dict:
    keys = jax.random.split(jax.random.key(seed), 8)
    kspace = noise(keys[0], (NY, ECHOES, COILS, RO, 2, NZ), 0.5, 3.0, ((1, 2), (2, 8), (3, 2)))
    sampling = plant((jax.random.randint(keys[1], (NY, ECHOES, NZ), 0, 3) < 1).astype(jnp.int32), jax.random.fold_in(keys[1], 1), 0, 1)
    coil_maps = noise(keys[2], (NY, COILS, RO, 2, NZ), 0.25, 1.5, ((1, 8), (2, 2)))
    image = noise(keys[3], (NY, ECHOES, RO, 2, NZ), 1.0, 6.0, ((0, 8), (1, 2), (2, 2)), jnp.float32)
    filters = noise(keys[4], (FILTERS, 3, 3, 3, 2), 54 ** -0.5, 0.875)
    thresholds = jnp.clip(jnp.exp(jax.random.uniform(keys[5], (FILTERS,), jnp.float32, math.log(0.5), math.log(8.0))), 0.5, 8.0)
    dc_weight = jnp.clip(jnp.exp(math.log(2.0) - 1.3862944 * jax.random.uniform(keys[6], (ECHOES,), jnp.float32) ** shard_levels(keys[6], (ECHOES,), ((0, 2),), -0.2, 0.2)), 0.5, 2.0)
    return {"kspace": kspace, "sampling": sampling, "coil_maps": coil_maps, "image": image, "filters": filters, "thresholds": thresholds, "dc_weight": dc_weight}


def tables(length):
    positions = jnp.arange(length, dtype=jnp.int32)
    product = positions[:, None] * positions[None, :] % length
    phases = product.astype(jnp.float32) * (2.0 * jnp.pi / length)
    normalize = length ** (-0.5)
    return (jnp.cos(phases) * normalize, jnp.sin(phases) * normalize)

def complex_times(left, right, conjugate):
    left_real = left[..., 0, :]
    left_imag = left[..., 1, :]
    right_real = right[..., 0, :]
    right_imag = right[..., 1, :]
    if conjugate:
        return jnp.stack([left_real * right_real + left_imag * right_imag, left_real * right_imag - left_imag * right_real], -2)
    return jnp.stack([left_real * right_real - left_imag * right_imag, left_real * right_imag + left_imag * right_real], -2)

def column_section(values, block):
    shape = values.shape
    merged = values.reshape(shape[:-2] + (shape[-2] * shape[-1],)).astype(jnp.float32)
    result = jnp.dot(merged, block.astype(jnp.float32))
    return result.reshape(shape)

def row_section(values, row_table, adjoint):
    lines = values.shape[0]
    result = jnp.einsum('ay,y...->a...', row_table.astype(jnp.float32), values.astype(jnp.float32))
    cosine_part = result[:lines]
    sine_part = result[lines:]
    if adjoint:
        return jnp.stack([cosine_part[..., 0, :] - sine_part[..., 1, :], cosine_part[..., 1, :] + sine_part[..., 0, :]], -2)
    return jnp.stack([cosine_part[..., 0, :] + sine_part[..., 1, :], cosine_part[..., 1, :] - sine_part[..., 0, :]], -2)

def reference(kspace, sampling, coil_maps, image, filters, thresholds, dc_weight):
    row_cos, row_sin = tables(NY)
    row_table = jnp.concatenate([row_cos, row_sin], 0).astype(jnp.bfloat16)
    col_cos, col_sin = tables(NZ)
    forward_block = jnp.block([[col_cos, -col_sin], [col_sin, col_cos]]).astype(jnp.bfloat16)
    adjoint_block = jnp.block([[col_cos, col_sin], [-col_sin, col_cos]]).astype(jnp.bfloat16)
    rounded = image.astype(jnp.bfloat16)
    sampled = sampling.astype(jnp.float32)[:, :, None, None, :]

    def per_coil(summed, coil_index):
        sensitivity = lax.dynamic_index_in_dim(coil_maps, coil_index, 1, keepdims=False).astype(jnp.float32)
        measured = lax.dynamic_index_in_dim(kspace, coil_index, 2, keepdims=False).astype(jnp.float32)
        weighted = complex_times(sensitivity[:, None], rounded.astype(jnp.float32), False).astype(jnp.bfloat16)
        halfway = column_section(weighted, forward_block).astype(jnp.bfloat16)
        spectrum = row_section(halfway, row_table, False)
        residual = (sampled * (spectrum - measured)).astype(jnp.bfloat16)
        backward = row_section(residual, row_table, True).astype(jnp.bfloat16)
        restored = column_section(backward, adjoint_block)
        return (summed + complex_times(sensitivity[:, None], restored, True), None)
    adjoint, _ = lax.scan(per_coil, jnp.zeros(image.shape, jnp.float32), jnp.arange(COILS, dtype=jnp.int32))
    padded = jnp.pad(rounded, ((1, 1), (0, 0), (1, 1), (0, 0), (1, 1))).astype(jnp.float32)
    lines, echoes, slices, parts, columns = image.shape

    def per_filter(summed, filter_pair):
        kernel, threshold = filter_pair
        kernel = kernel.astype(jnp.float32)
        response = jnp.zeros((lines, echoes, slices, columns), jnp.float32)
        for shift_y in range(3):
            for shift_r in range(3):
                for shift_z in range(3):
                    window = padded[shift_y:shift_y + lines, :, shift_r:shift_r + slices, :, shift_z:shift_z + columns]
                    response = response + kernel[shift_y, shift_r, shift_z, 0] * window[:, :, :, 0] + kernel[shift_y, shift_r, shift_z, 1] * window[:, :, :, 1]
        magnitude = jnp.sqrt(lax.optimization_barrier(jnp.sum(response * response, axis=1)))
        factor = magnitude / (magnitude + threshold)
        shrunk = (response * factor[:, None]).astype(jnp.bfloat16).astype(jnp.float32)
        shrunk_pad = jnp.pad(shrunk, ((1, 1), (0, 0), (1, 1), (1, 1)))
        contribution = jnp.zeros(image.shape, jnp.float32)
        for shift_y in range(3):
            for shift_r in range(3):
                for shift_z in range(3):
                    window = shrunk_pad[2 - shift_y:2 - shift_y + lines, :, 2 - shift_r:2 - shift_r + slices, 2 - shift_z:2 - shift_z + columns]
                    contribution = contribution + jnp.stack([kernel[shift_y, shift_r, shift_z, 0] * window, kernel[shift_y, shift_r, shift_z, 1] * window], -2)
        return (summed + contribution, None)
    penalty, _ = lax.scan(per_filter, jnp.zeros(image.shape, jnp.float32), (filters, thresholds))
    return image - dc_weight[None, :, None, None, None] * adjoint - penalty
```

```python
import functools

import numpy as np
import jax
import jax.numpy as jnp
from jax import lax
from jax.experimental import pallas as pl
from jax.experimental.pallas import tpu as pltpu
from jax.sharding import PartitionSpec as P

MESH = pl.DeviceIdType.MESH
F32 = jnp.float32
BF16 = jnp.bfloat16
SLAB = 32
GRANT = 24 << 20


def tables(length):
    product = np.outer(np.arange(length), np.arange(length)) % length
    phases = product * (2.0 * np.pi / length)
    normalize = length ** (-0.5)
    return np.cos(phases) * normalize, np.sin(phases) * normalize


def window_rows(rows, peers):
    for size in range(2, rows + 1):
        if rows % size == 0 and rows // size <= peers:
            return size
    return rows


def dot(left, right):
    return jnp.dot(left, right, preferred_element_type=F32)


def kernel(
    cfg,
    image_hbm, spread_hbm, filters_hbm, thr_hbm, dc_ref, kspace_hbm, maps_hbm, samp_hbm, fz_hbm, az_hbm, ty_hbm,
    out_ref,
    image, flat, padded, spread, filters, thr,
    gat, part, paired, rs_send, rs_recv, wide_ref, tall_ref, level, ext, edge, pen_send, pen_recv, pacc, slab,
    kspace, maps, samp, fz, az, ty,
    local_sem, ag_send_sem, ag_recv_sem, x_send_sem, x_recv_sem, e_send_sem, e_recv_sem,
    p_send_sem, p_recv_sem, rs_send_sem, rs_recv_sem, f_send_sem, f_recv_sem, pair_send_sem, pair_recv_sem,
):
    n_e, n_c, n_r, n_q, rq, nz, ny = cfg
    peers = n_e * n_r
    e = lax.axis_index("echo")
    c = lax.axis_index("coil")
    r = lax.axis_index("read")
    q = e * n_r + r
    s_local, rb = rs_send.shape[0], flat.shape[0]
    chips = n_c // 2
    core = lax.rem(c, 2)
    chip = c // 2
    partner = c + 1 - 2 * core
    width = 2 * nz
    zp = ext.shape[-1]

    loads = [
        pltpu.make_async_copy(src, dst, local_sem.at[i])
        for i, (src, dst) in enumerate(
            [
                (image_hbm, image), (spread_hbm, spread), (filters_hbm, filters), (thr_hbm, thr),
                (maps_hbm, maps), (fz_hbm, fz), (ty_hbm, ty), (kspace_hbm, kspace), (samp_hbm, samp), (az_hbm, az),
            ]
        )
    ]

    for load in loads:
        load.start()

    def remote(src, dst, send, recv, target):
        return pltpu.make_async_remote_copy(
            src_ref=src, dst_ref=dst, send_sem=send, recv_sem=recv, device_id=target, device_id_type=MESH
        )

    def when(condition, act):
        if condition is True:
            act()
        else:
            pl.when(condition)(act)

    def up(d):
        return lax.rem(q + d, peers)

    def down(d):
        return lax.rem(q + peers - d, peers)

    def active(which):
        return True if n_q == peers else which < n_q

    barrier = pltpu.get_barrier_semaphore()
    for d in range(chips):
        to = lax.rem(c + 2 * d, n_c) if d else partner
        pl.semaphore_signal(barrier, inc=1, device_id=(e, to, r), device_id_type=MESH)
    for d in range(peers):
        if d:
            pl.semaphore_signal(barrier, inc=1, device_id=(up(d) // n_r, c, lax.rem(up(d), n_r)), device_id_type=MESH)
        for step, ok in ((1, c < n_c - 1), (-1, c > 0)):
            @pl.when(ok)
            def _():
                pl.semaphore_signal(
                    barrier, inc=1, device_id=(up(d) // n_r, c + step, lax.rem(up(d), n_r)), device_id_type=MESH
                )
    margin = rq + 2
    padded[...] = jnp.zeros_like(padded)
    loads[0].wait()
    flat[...] = jnp.concatenate([image[:, s, p, :] for s in range(s_local) for p in range(2)], axis=1)
    gat[c] = flat[...].astype(BF16)
    padded[margin : margin + rb, :, :nz] = image[...].reshape(rb, 2 * s_local, nz).astype(BF16)

    sides = jnp.minimum(c, 1) + jnp.minimum(n_c - 1 - c, 1)
    pl.semaphore_wait(barrier, chips + peers - 1 + peers * sides)

    def window(d):
        to = up(d)
        return remote(
            padded.at[pl.ds((1 + to) * rq, rq + 4)], ext.at[e, r], x_send_sem.at[d], x_recv_sem.at[d], (to // n_r, c, lax.rem(to, n_r))
        )

    last = n_q - 1
    edge_up = lambda: remote(
        padded.at[pl.ds((n_q + 1) * rq, rq + 4)], edge.at[e, r], e_send_sem.at[0], e_recv_sem.at[q], (0, c + 1, 0)
    )
    edge_down = lambda: remote(
        padded.at[pl.ds(0, rq + 4)], edge.at[e, r], e_send_sem.at[1], e_recv_sem.at[q], (last // n_r, c - 1, last % n_r)
    )
    for d in range(1, peers):
        when(active(up(d)), lambda: window(d).start())
    pl.when(c < n_c - 1)(lambda: edge_up().start())
    pl.when(c > 0)(lambda: edge_down().start())

    def gather(d):
        to = lax.rem(c + 2 * d, n_c) if d else partner
        return remote(gat.at[c], gat.at[c], ag_send_sem.at[d], ag_recv_sem.at[d], (e, to, r))

    def forward(d):
        src = lax.rem(c + n_c - 2 * d, n_c)
        return remote(gat.at[src], gat.at[src], f_send_sem.at[d], f_recv_sem.at[d], (e, partner, r))

    for d in range(chips):
        gather(d).start()

    count = filters.shape[-1]
    slices = s_local * n_r
    for load in loads[1:4]:
        load.wait()
    flat_filters = filters[...].astype(F32).reshape(-1, count).astype(BF16)
    pieces = [dot(spread[at], flat_filters) for at in range(slices)]
    for at in range(slices):
        wide_ref[:, at * count : (at + 1) * count] = pieces[at].astype(BF16)
        tall_ref[at * count : (at + 1) * count, :] = pieces[at].T.astype(BF16)
    shape = (slices, count, count)
    on = lax.broadcasted_iota(jnp.int32, shape, 1) == lax.broadcasted_iota(jnp.int32, shape, 2)
    column = jnp.sum(jnp.where(on, thr[...].reshape(1, 1, count), 0.0), axis=2, keepdims=True)
    level[...] = jnp.broadcast_to(column, (slices, count, zp)).reshape(slices * count, zp)

    has_edge = jnp.logical_or(
        jnp.logical_and(q == 0, c > 0), jnp.logical_and(q == last, c < n_c - 1)
    )

    @pl.when(jnp.logical_not(has_edge))
    def _():
        edge[...] = jnp.zeros_like(edge)

    def prepare():
        ext[e, r] = padded[pl.ds((1 + q) * rq, rq + 4)]
        for d in range(1, peers):
            src = down(d)
            remote(
                padded.at[pl.ds(0, rq + 4)], ext.at[src // n_r, lax.rem(src, n_r)], x_send_sem.at[d], x_recv_sem.at[d], (e, c, r)
            ).wait_recv()

        @pl.when(has_edge)
        def _():
            for src in range(peers):
                remote(
                    padded.at[pl.ds(0, rq + 4)], edge.at[src // n_r, src % n_r], e_send_sem.at[0], e_recv_sem.at[src], (e, c, r)
                ).wait_recv()

        rows = rq + 4
        taps = 2 * s_local * n_r
        for echo in range(n_e):
            parts = [ext[echo, read].astype(F32) + edge[echo, read].astype(F32) for read in range(n_r)]
            block = jnp.concatenate(parts, axis=1) if n_r > 1 else parts[0]
            flat = block.reshape(rows * taps, zp)
            moved = [
                pltpu.roll(flat, 1, 1).reshape(rows, taps, zp),
                block,
                pltpu.roll(flat, zp - 1, 1).reshape(rows, taps, zp),
            ]
            fill = [jnp.zeros((rows, SLAB - 3 * taps, zp), F32)] if SLAB > 3 * taps else []
            slab[echo] = jnp.concatenate(moved + fill, axis=1).reshape(rows * SLAB, zp).astype(BF16)

        pacc[...] = jnp.zeros_like(pacc)

    def respond(begin, end):
        tall = tall_ref[...]
        wide = wide_ref[...]
        lane_ok = lax.broadcasted_iota(jnp.int32, (1, zp), 1) < nz
        first = c * rb + q * rq - 1

        def row(i, carry):
            start = pl.multiple_of(i * SLAB, SLAB)
            response = [dot(tall, slab[echo, pl.ds(start, 3 * SLAB), :]) for echo in range(n_e)]
            energy = response[0] * response[0]
            for other in response[1:]:
                energy = energy + other * other
            magnitude = jnp.sqrt(energy)
            factor = magnitude / (magnitude + level[...])
            inside = jnp.logical_and(first + i >= 0, first + i < ny)
            factor = jnp.where(jnp.logical_and(lane_ok, inside), factor, 0.0)
            for echo in range(n_e):
                spread = dot(wide, (response[echo] * factor).astype(BF16))
                for a in range(3):
                    pacc[echo, i + a] += spread[a * SLAB : (a + 1) * SLAB]
            return carry

        lax.fori_loop(begin, end, row, 0, unroll=True)

    def collect():
        taps = 2 * s_local * n_r
        for echo in range(n_e):
            held = pacc[echo, 2 : 2 + rq]
            low = pltpu.roll(held[:, :taps].reshape(rq * taps, zp), zp - 1, 1).reshape(rq, taps, zp)
            high = pltpu.roll(held[:, 2 * taps : 3 * taps].reshape(rq * taps, zp), 1, 1).reshape(rq, taps, zp)
            total = low + held[:, taps : 2 * taps] + high
            for read in range(n_r):
                pen_send[echo, read] = total[:, read * 2 * s_local : (read + 1) * 2 * s_local]
        pen_recv[q] = pen_send[e, r]

    def penalty_out(d):
        to = up(d)
        return remote(
            pen_send.at[to // n_r, lax.rem(to, n_r)], pen_recv.at[q], p_send_sem.at[d], p_recv_sem.at[d],
            (to // n_r, c, lax.rem(to, n_r)),
        )

    split = (rq + 2) * 2 // 3

    def before():
        prepare()
        respond(0, split)

    def after():
        respond(split, rq + 2)
        collect()
        for d in range(1, peers):
            penalty_out(d).start()

    when(active(q), before)

    for d in range(1, chips):
        src = lax.rem(c + n_c - 2 * d, n_c)
        remote(gat.at[src], gat.at[src], ag_send_sem.at[d], ag_recv_sem.at[d], (e, partner, r)).wait_recv()
        forward(d).start()
    remote(gat.at[partner], gat.at[partner], ag_send_sem.at[0], ag_recv_sem.at[0], (e, partner, r)).wait_recv()
    for d in range(1, chips):
        src = lax.rem(partner + n_c - 2 * d, n_c)
        remote(gat.at[src], gat.at[src], f_send_sem.at[d], f_recv_sem.at[d], (e, partner, r)).wait_recv()
    for load in loads[4:]:
        load.wait()

    def pair(s):
        return remote(
            part.at[s, :, 1 - core], paired.at[s], pair_send_sem.at[s], pair_recv_sem.at[s], (e, partner, r)
        )

    def scatter(s, d):
        to = lax.rem(chip + d, chips)
        return remote(
            rs_send.at[s, to], rs_recv.at[s, chip], rs_send_sem.at[s, d], rs_recv_sem.at[s, d],
            (e, 2 * to + core, r),
        )

    def send_sums(s):
        pair(s).wait_recv()
        rs_send[s] = (part[s, :, core].astype(F32) + paired[s].astype(F32)).astype(BF16)
        for d in range(1, chips):
            scatter(s, d).start()

    sampled = samp[...].astype(F32)
    for s in range(s_local):
        image = gat[:, :, s * width : (s + 1) * width].astype(F32).reshape(ny, width).T
        real, imag = image[:nz], image[nz:]
        map_real, map_imag = maps[s, 0].astype(F32), maps[s, 1].astype(F32)
        weighted = jnp.concatenate(
            [map_real * real - map_imag * imag, map_real * imag + map_imag * real], 0
        ).astype(BF16)
        halfway = dot(fz[...], weighted).astype(BF16)
        spectrum = dot(halfway, ty[...])
        if s:
            send_sums(s - 1)
        spec_real = spectrum[:nz, :ny] + spectrum[nz:, ny:]
        spec_imag = spectrum[nz:, :ny] - spectrum[:nz, ny:]
        residual = jnp.concatenate(
            [
                sampled * (spec_real - kspace[s, 0].astype(F32)),
                sampled * (spec_imag - kspace[s, 1].astype(F32)),
            ],
            0,
        ).astype(BF16)
        returned = dot(residual, ty[...])
        backward = jnp.concatenate(
            [returned[:nz, :ny] - returned[nz:, ny:], returned[nz:, :ny] + returned[:nz, ny:]], 0
        ).astype(BF16)
        restored = dot(az[...], backward)
        back_real, back_imag = restored[:nz], restored[nz:]
        map_real, map_imag = maps[s, 0].astype(F32), maps[s, 1].astype(F32)
        adjoint = jnp.concatenate(
            [map_real * back_real + map_imag * back_imag, map_real * back_imag - map_imag * back_real], 0
        ).T
        part[s] = adjoint.reshape(chips, 2, rb, width).astype(BF16)
        pair(s).start()
    send_sums(s_local - 1)
    when(active(q), after)

    for d in range(1, peers):
        src = down(d)
        when(
            active(src),
            lambda: remote(
                pen_send.at[0, 0], pen_recv.at[src], p_send_sem.at[d], p_recv_sem.at[d], (e, c, r)
            ).wait_recv(),
        )
    held = pen_recv[...].reshape(rb, 2 * s_local, zp)
    base = flat[...] - jnp.concatenate([held[:, k, :nz] for k in range(2 * s_local)], axis=1)
    for s in range(s_local):
        total = part[s, chip, core].astype(F32) + paired[s, chip].astype(F32)
        for d in range(1, chips):
            src = lax.rem(chip + chips - d, chips)
            remote(
                rs_send.at[s, src], rs_recv.at[s, src], rs_send_sem.at[s, d], rs_recv_sem.at[s, d], (e, partner, r)
            ).wait_recv()
            total = total + rs_recv[s, src].astype(F32)
        out_ref[:, s * width : (s + 1) * width] = base[:, s * width : (s + 1) * width] - dc_ref[0] * total

    for d in range(chips):
        gather(d).wait_send()
        if d:
            forward(d).wait_send()
            for s in range(s_local):
                scatter(s, d).wait_send()
    for s in range(s_local):
        pair(s).wait_send()
    for d in range(1, peers):
        when(active(up(d)), lambda: window(d).wait_send())
        when(active(q), lambda: penalty_out(d).wait_send())
    pl.when(c < n_c - 1)(lambda: edge_up().wait_send())
    pl.when(c > 0)(lambda: edge_down().wait_send())


def body(kspace, sampling, coil_maps, image, filters, thresholds, dc_weight):
    n_e, n_c, n_r = lax.axis_size("echo"), lax.axis_size("coil"), lax.axis_size("read")
    rb, _, s_local, _, nz = image.shape
    ny = kspace.shape[0]
    peers = n_e * n_r
    rq = window_rows(rb, peers)
    n_q = rb // rq
    zp = -(-(nz + 1) // 128) * 128
    width = 2 * nz
    slices = s_local * n_r
    taps = 2 * slices
    count = filters.shape[0]

    col_cos, col_sin = tables(nz)
    row_cos, row_sin = tables(ny)
    fz = jnp.asarray(np.block([[col_cos, col_sin], [-col_sin, col_cos]]), BF16)
    az = jnp.asarray(np.block([[col_cos, -col_sin], [col_sin, col_cos]]), BF16)
    ty = jnp.asarray(np.concatenate([row_cos, row_sin], 1), BF16)

    spread = np.zeros((slices, 3, SLAB, 3, 3, 3, 2))
    for at in range(slices):
        for a in range(3):
            for b in range(3):
                for d in range(3):
                    for p in range(2):
                        if 0 <= at + b - 1 < slices:
                            spread[at, a, d * taps + (at + b - 1) * 2 + p, a, b, d, p] = 1.0
    spread = jnp.asarray(spread.reshape(slices, 3 * SLAB, 54), BF16)

    k_view = jnp.transpose(kspace[:, 0, 0], (1, 2, 3, 0))
    m_view = jnp.transpose(coil_maps[:, 0], (1, 2, 3, 0))
    s_view = jnp.transpose(sampling[:, 0], (1, 0))

    operands = tuple(
        pltpu.with_memory_space_constraint(x, pltpu.HBM)
        for x in (
            image[:, 0], spread, jnp.transpose(filters, (1, 2, 3, 4, 0)), thresholds[None, :],
            k_view, m_view, s_view, fz, az, ty,
        )
    )
    vmem = pl.BlockSpec(memory_space=pltpu.VMEM)
    hbm = pl.BlockSpec(memory_space=pltpu.HBM)
    smem = pl.BlockSpec(memory_space=pltpu.SMEM)
    dma = pltpu.SemaphoreType.DMA
    updated = pl.pallas_call(
        functools.partial(kernel, (n_e, n_c, n_r, n_q, rq, nz, ny)),
        out_shape=jax.ShapeDtypeStruct((rb, s_local * width), F32),
        in_specs=[hbm] * 4 + [smem] + [hbm] * 6,
        out_specs=vmem,
        scratch_shapes=[
            pltpu.VMEM((rb, s_local, 2, nz), F32),
            pltpu.VMEM((rb, s_local * width), F32),
            pltpu.VMEM((rb + 2 * (rq + 2), 2 * s_local, zp), BF16),
            pltpu.VMEM(spread.shape, BF16),
            pltpu.VMEM((3, 3, 3, 2, count), BF16),
            pltpu.VMEM((1, count), F32),
            pltpu.VMEM((n_c, rb, s_local * width), BF16),
            pltpu.VMEM((s_local, n_c // 2, 2, rb, width), BF16),
            pltpu.VMEM((s_local, n_c // 2, rb, width), BF16),
            pltpu.VMEM((s_local, n_c // 2, rb, width), BF16),
            pltpu.VMEM((s_local, n_c // 2, rb, width), BF16),
            pltpu.VMEM((3 * SLAB, slices * count), BF16),
            pltpu.VMEM((slices * count, 3 * SLAB), BF16),
            pltpu.VMEM((slices * count, zp), F32),
            pltpu.VMEM((n_e, n_r, rq + 4, 2 * s_local, zp), BF16),
            pltpu.VMEM((n_e, n_r, rq + 4, 2 * s_local, zp), BF16),
            pltpu.VMEM((n_e, n_r, rq, 2 * s_local, zp), F32),
            pltpu.VMEM((n_q, rq, 2 * s_local, zp), F32),
            pltpu.VMEM((n_e, rq + 4, SLAB, zp), F32),
            pltpu.VMEM((n_e, (rq + 4) * SLAB, zp), BF16),
            pltpu.VMEM(k_view.shape, BF16),
            pltpu.VMEM(m_view.shape, BF16),
            pltpu.VMEM(s_view.shape, jnp.int32),
            pltpu.VMEM(fz.shape, BF16),
            pltpu.VMEM(az.shape, BF16),
            pltpu.VMEM(ty.shape, BF16),
            dma((10,)),
            dma((n_c,)), dma((n_c,)),
            dma((peers,)), dma((peers,)),
            dma((2,)), dma((peers,)),
            dma((peers,)), dma((peers,)),
            dma((s_local, n_c)), dma((s_local, n_c)),
            dma((n_c,)), dma((n_c,)), dma((s_local,)), dma((s_local,)),
        ],
        compiler_params=pltpu.CompilerParams(
            collective_id=0, has_side_effects=True, vmem_limit_bytes=GRANT
        ),
        name="cascade",
    )(*operands[:4], dc_weight, *operands[4:])
    return updated.reshape(image.shape)


def solution(mesh):
    return jax.shard_map(
        body,
        mesh=mesh,
        in_specs=(
            P(None, "echo", "coil", "read", None, None),
            P(None, "echo", None),
            P(None, "coil", "read", None, None),
            P("coil", "echo", "read", None, None),
            P(),
            P(),
            P("echo"),
        ),
        out_specs=P("coil", "echo", "read", None, None),
        check_vma=False,
    )
```

```python
import functools

import numpy as np
import jax
import jax.numpy as jnp
from jax import lax
from jax.experimental import pallas as pl
from jax.experimental.pallas import tpu as pltpu
from jax.sharding import PartitionSpec as P

MESH = pl.DeviceIdType.MESH
F32 = jnp.float32
BF16 = jnp.bfloat16
SLAB = 32
GRANT = 24 << 20
TINY = float(np.finfo(np.float32).tiny)
SPLITS = (3, 8, 10, 11)


def tables(length):
    product = np.outer(np.arange(length), np.arange(length)) % length
    phases = product * (2.0 * np.pi / length)
    normalize = length ** (-0.5)
    return np.cos(phases) * normalize, np.sin(phases) * normalize


def window_rows(rows, peers):
    for size in range(2, rows + 1):
        if rows % size == 0 and rows // size <= peers:
            return size
    return rows


def dot(left, right):
    return jnp.dot(left, right, preferred_element_type=F32)


def kernel(
    cfg,
    image_hbm, spread_hbm, filters_hbm, thr_hbm, dc_ref, kspace_hbm, maps_hbm, samp_hbm, fz_hbm, az_hbm, ty_hbm,
    out_ref,
    image, flat, padded, spread, filters, thr,
    gat, part, paired, rs_send, rs_recv, wide_ref, tall_ref, level, ext, edge, pen_send, pen_recv, pacc, slab,
    kspace, maps, samp, fz, az, ty, k_rows, m_rows, s_rows, weighted, stack,
    local_sem, ag_send_sem, ag_recv_sem, x_send_sem, x_recv_sem, e_send_sem, e_recv_sem,
    p_send_sem, p_recv_sem, rs_send_sem, rs_recv_sem, f_send_sem, f_recv_sem, pair_send_sem, pair_recv_sem,
):
    n_e, n_c, n_r, n_q, rq, nz, ny = cfg
    peers = n_e * n_r
    e = lax.axis_index("echo")
    c = lax.axis_index("coil")
    r = lax.axis_index("read")
    q = e * n_r + r
    s_local, rb = rs_send.shape[0], flat.shape[0]
    chips = n_c // 2
    core = lax.rem(c, 2)
    chip = c // 2
    partner = c + 1 - 2 * core
    width = 2 * nz
    zp = ext.shape[-1]
    half = ny // 2
    group = chips // 2
    side = jnp.where(chip < group, 1, 0)

    loads = [
        pltpu.make_async_copy(src, dst, local_sem.at[i])
        for i, (src, dst) in enumerate(
            [
                (image_hbm, image), (spread_hbm, spread), (filters_hbm, filters), (thr_hbm, thr),
                (maps_hbm, maps), (fz_hbm, fz), (ty_hbm, ty), (kspace_hbm, kspace), (samp_hbm, samp), (az_hbm, az),
            ]
        )
    ]

    for load in loads:
        load.start()

    def remote(src, dst, send, recv, target):
        return pltpu.make_async_remote_copy(
            src_ref=src, dst_ref=dst, send_sem=send, recv_sem=recv, device_id=target, device_id_type=MESH
        )

    def when(condition, act):
        if condition is True:
            act()
        else:
            pl.when(condition)(act)

    def up(d):
        return lax.rem(q + d, peers)

    def down(d):
        return lax.rem(q + peers - d, peers)

    def active(which):
        return True if n_q == peers else which < n_q

    barrier = pltpu.get_barrier_semaphore()
    for d in range(chips):
        to = lax.rem(c + 2 * d, n_c) if d else partner
        pl.semaphore_signal(barrier, inc=1, device_id=(e, to, r), device_id_type=MESH)
    for d in range(peers):
        if d:
            pl.semaphore_signal(barrier, inc=1, device_id=(up(d) // n_r, c, lax.rem(up(d), n_r)), device_id_type=MESH)
        for step, ok in ((1, c < n_c - 1), (-1, c > 0)):
            @pl.when(ok)
            def _():
                pl.semaphore_signal(
                    barrier, inc=1, device_id=(up(d) // n_r, c + step, lax.rem(up(d), n_r)), device_id_type=MESH
                )
    margin = rq + 2
    loads[0].wait()
    flat[...] = jnp.concatenate([image[:, s, p, :] for s in range(s_local) for p in range(2)], axis=1)
    for s in range(s_local):
        gat[s, c] = flat[:, s * width : (s + 1) * width].astype(BF16)

    sides = jnp.minimum(c, 1) + jnp.minimum(n_c - 1 - c, 1)
    pl.semaphore_wait(barrier, chips + peers - 1 + peers * sides)

    def window(d):
        to = up(d)
        return remote(
            padded.at[pl.ds((1 + to) * rq, rq + 4)], ext.at[e, r], x_send_sem.at[d], x_recv_sem.at[d], (to // n_r, c, lax.rem(to, n_r))
        )

    last = n_q - 1
    def edge_up():
        return remote(
            padded.at[pl.ds(margin + rb - 2, 2)], edge.at[0, e, r], e_send_sem.at[0], e_recv_sem.at[0, q], (0, c + 1, 0)
        )

    def edge_down():
        return remote(
            padded.at[pl.ds(margin, 2)], edge.at[1, e, r], e_send_sem.at[1], e_recv_sem.at[1, q],
            (last // n_r, c - 1, last % n_r),
        )

    def gather(s, d):
        to = lax.rem(c + 2 * d, n_c) if d is not None else partner
        at = 0 if d is None else d
        return remote(gat.at[s, c], gat.at[s, c], ag_send_sem.at[s, at], ag_recv_sem.at[s, at], (e, to, r))

    def gathered(s, d):
        src = lax.rem(c + n_c - 2 * d, n_c)
        return remote(gat.at[s, src], gat.at[s, src], ag_send_sem.at[s, d], ag_recv_sem.at[s, d], (e, partner, r))

    def forward(s, d):
        src = lax.rem(c + n_c - 2 * d, n_c)
        return remote(gat.at[s, src], gat.at[s, src], f_send_sem.at[s, d], f_recv_sem.at[s, d], (e, partner, r))

    def targets(act, dists):
        for dist in dists:
            pl.when(chip + dist < chips)(lambda: act(dist))
            pl.when(chip - dist >= 0)(lambda: act(chips - dist))

    def relay(s, dists):
        def one(d):
            gathered(s, d).wait_recv()
            forward(s, d).start()

        for dist in dists:
            pl.when(chip - dist >= 0)(lambda: one(dist))
            pl.when(chip + dist < chips)(lambda: one(chips - dist))

    near = range(1, chips)
    far = near[::-1]

    padded[...] = jnp.zeros_like(padded)
    padded[margin : margin + rb, :, :nz] = image[...].reshape(rb, 2 * s_local, nz).astype(BF16)
    for d in range(1, peers):
        when(active(up(d)), lambda: window(d).start())
    pl.when(c < n_c - 1)(lambda: edge_up().start())
    pl.when(c > 0)(lambda: edge_down().start())
    for s in range(s_local):
        targets(lambda d: gather(s, d).start(), near if s else far)
        gather(s, None).start()

    def complete(s):
        remote(
            gat.at[s, partner], gat.at[s, partner], ag_send_sem.at[s, 0], ag_recv_sem.at[s, 0], (e, partner, r)
        ).wait_recv()
        for d in range(1, chips):
            src = lax.rem(partner + n_c - 2 * d, n_c)
            remote(
                gat.at[s, src], gat.at[s, src], f_send_sem.at[s, d], f_recv_sem.at[s, d], (e, partner, r)
            ).wait_recv()

    count = filters.shape[-1]
    slices = s_local * n_r
    for load in loads[1:4]:
        load.wait()
    flat_filters = filters[...].astype(F32).reshape(-1, count).astype(BF16)
    pieces = [dot(spread[at], flat_filters) for at in range(slices)]
    for at in range(slices):
        wide_ref[:, at * count : (at + 1) * count] = pieces[at].astype(BF16)
        tall_ref[at * count : (at + 1) * count, :] = pieces[at].T.astype(BF16)
    shape = (slices, count, count)
    on = lax.broadcasted_iota(jnp.int32, shape, 1) == lax.broadcasted_iota(jnp.int32, shape, 2)
    column = jnp.sum(jnp.where(on, thr[...].reshape(1, 1, count), 0.0), axis=2, keepdims=True)
    level[...] = jnp.broadcast_to(column, (slices, count, zp)).reshape(slices * count, zp)

    def prepare():
        ext[e, r] = padded[pl.ds((1 + q) * rq, rq + 4)]
        for d in range(1, peers):
            src = down(d)
            remote(
                padded.at[pl.ds(0, rq + 4)], ext.at[src // n_r, lax.rem(src, n_r)], x_send_sem.at[d], x_recv_sem.at[d], (e, c, r)
            ).wait_recv()

        def border(which, begin):
            for src in range(peers):
                at = (which, src // n_r, src % n_r)
                remote(
                    padded.at[pl.ds(0, 2)], edge.at[at], e_send_sem.at[0], e_recv_sem.at[which, src], (e, c, r)
                ).wait_recv()
                ext[src // n_r, src % n_r, begin : begin + 2] = edge[at]

        pl.when(jnp.logical_and(q == 0, c > 0))(lambda: border(0, 0))
        pl.when(jnp.logical_and(q == last, c < n_c - 1))(lambda: border(1, rq + 2))

        rows = rq + 4
        taps = 2 * s_local * n_r
        for echo in range(n_e):
            parts = [ext[echo, read].astype(F32) for read in range(n_r)]
            block = jnp.concatenate(parts, axis=1) if n_r > 1 else parts[0]
            flat = block.reshape(rows * taps, zp)
            moved = [
                pltpu.roll(flat, 1, 1).reshape(rows, taps, zp),
                block,
                pltpu.roll(flat, zp - 1, 1).reshape(rows, taps, zp),
            ]
            fill = [jnp.zeros((rows, SLAB - 3 * taps, zp), F32)] if SLAB > 3 * taps else []
            slab[echo] = jnp.concatenate(moved + fill, axis=1).reshape(rows * SLAB, zp).astype(BF16)

        pacc[...] = jnp.zeros_like(pacc)

    def respond(begin, end):
        tall = tall_ref[...]
        wide = wide_ref[...]
        first = c * rb + q * rq - 1

        for i in range(begin, end):
            window = slice(i * SLAB, (i + 3) * SLAB)
            response = [dot(tall, slab[echo, window, :]) for echo in range(n_e)]
            energy = response[0] * response[0]
            for other in response[1:]:
                energy = energy + other * other
            factor = 1.0 / (1.0 + level[...] * lax.rsqrt(jnp.maximum(energy, TINY)))
            if i in (0, rq + 1):
                inside = jnp.logical_and(first + i >= 0, first + i < ny)
                factor = jnp.where(inside, factor, 0.0)
            for echo in range(n_e):
                spread = dot(wide, (response[echo] * factor).astype(BF16))
                for a in range(3):
                    pacc[echo, i + a] += spread[a * SLAB : (a + 1) * SLAB]

    def collect():
        taps = 2 * s_local * n_r
        lane = lax.broadcasted_iota(jnp.int32, (1, 1, zp), 2)
        for echo in range(n_e):
            held = pacc[echo, 2 : 2 + rq]
            low = pltpu.roll(held[:, :taps].reshape(rq * taps, zp), zp - 1, 1).reshape(rq, taps, zp)
            high = pltpu.roll(held[:, 2 * taps : 3 * taps].reshape(rq * taps, zp), 1, 1).reshape(rq, taps, zp)
            low = jnp.where(lane < nz - 1, low, 0.0)
            high = jnp.where(lane > 0, high, 0.0)
            total = low + held[:, taps : 2 * taps] + high
            for read in range(n_r):
                pen_send[echo, read] = total[:, read * 2 * s_local : (read + 1) * 2 * s_local].astype(BF16)
        pen_recv[q] = pen_send[e, r]

    def penalty_out(d):
        to = up(d)
        return remote(
            pen_send.at[to // n_r, lax.rem(to, n_r)], pen_recv.at[q], p_send_sem.at[d], p_recv_sem.at[d],
            (to // n_r, c, lax.rem(to, n_r)),
        )

    marks = [0] + [(rq + 2) * part // 14 for part in SPLITS] + [rq + 2]

    def rows(at):
        def act():
            if at == 0:
                prepare()
            respond(marks[at], marks[at + 1])
            if at == len(marks) - 2:
                collect()
                for d in range(1, peers):
                    penalty_out(d).start()

        when(active(q), act)

    def turn():
        for load in loads[4:]:
            load.wait()
        for buf in (k_rows, m_rows, weighted):
            buf[...] = jnp.zeros_like(buf)
        for s in range(s_local):
            for p in range(2):
                at = slice(p * zp, p * zp + nz)
                k_rows[s, :, at] = kspace[s, p].astype(F32).T.astype(BF16)
                m_rows[s, :, at] = maps[s, p].astype(F32).T.astype(BF16)
        s_rows[:, :nz] = samp[...].astype(F32).T
        s_rows[:, nz:] = jnp.zeros((ny, zp - nz), F32)

    def halves(j):
        return side if j == 0 else 1 - side

    def pair(s, j):
        h = halves(j)
        return remote(
            part.at[s, h, :, 1 - core], paired.at[s, h], pair_send_sem.at[s, j], pair_recv_sem.at[s, j],
            (e, partner, r),
        )

    def scatter(s, to):
        d = lax.rem(to - chip + chips, chips)
        return remote(
            rs_send.at[s, to], rs_recv.at[s, chip], rs_send_sem.at[s, d], rs_recv_sem.at[s, d],
            (e, 2 * to + core, r),
        )

    def send_sums(s, j):
        pair(s, j).wait_recv()
        h = halves(j)
        sums = (part[s, h, :, core].astype(F32) + paired[s, h].astype(F32)).astype(BF16)
        for k in range(group):
            to = h * group + k
            rs_send[s, to] = sums[k]
            if j:
                pl.when(to != chip)(lambda: scatter(s, to).start())
            else:
                scatter(s, to).start()

    def swapped(x, sign):
        low, high = x[:, :zp], x[:, zp:]
        return jnp.concatenate([high, -low] if sign > 0 else [-high, low], axis=1)

    def columns(s, which):
        starts = [pl.multiple_of((2 * k + which) * rb, 8) for k in range(chips)]
        image = jnp.concatenate([gat[s, 2 * k + which] for k in range(chips)], axis=0)
        sense = jnp.concatenate([m_rows[s, pl.ds(at, rb), :] for at in starts], axis=0)
        real, imag = image[:, :nz].astype(F32), image[:, nz:].astype(F32)
        map_real, map_imag = sense[:, :nz].astype(F32), sense[:, zp : zp + nz].astype(F32)
        weighted[:half, :nz] = (map_real * real - map_imag * imag).astype(BF16)
        weighted[:half, zp : zp + nz] = (map_real * imag + map_imag * real).astype(BF16)
        halfway = dot(weighted[:half, :], fz[...])
        upper, lower = halfway.astype(BF16), swapped(halfway, 1).astype(BF16)
        for k, at in enumerate(starts):
            stack[pl.ds(at, rb), :] = upper[k * rb : (k + 1) * rb]
            stack[pl.ds(ny + at, rb), :] = lower[k * rb : (k + 1) * rb]

    def fronts(s):
        spectrum = dot(ty[...], stack[...])
        sampled = s_rows[...]
        sampled = jnp.concatenate([sampled, sampled], axis=1)
        residual = sampled * (spectrum - k_rows[s].astype(F32))
        stack[:ny] = residual.astype(BF16)
        stack[ny:] = swapped(residual, -1).astype(BF16)

    def middle():
        weighted[...] = dot(ty[...], stack[...]).astype(BF16)

    def backs(s, j):
        h = halves(j)
        at = pl.ds(pl.multiple_of(h * half, 16), half)
        restored = dot(weighted[at, :], az[...])
        back_real, back_imag = restored[:, :nz], restored[:, zp : zp + nz]
        map_real, map_imag = m_rows[s, at, :nz].astype(F32), m_rows[s, at, zp : zp + nz].astype(F32)
        adjoint = jnp.concatenate(
            [
                (map_real * back_real + map_imag * back_imag).astype(BF16),
                (map_real * back_imag - map_imag * back_real).astype(BF16),
            ],
            axis=1,
        )
        part[s, h] = adjoint.reshape(group, 2, rb, width)
        pair(s, j).start()

    turn()
    rows(0)
    rows(1)
    relay(0, near)
    columns(0, core)
    complete(0)
    columns(0, 1 - core)
    fronts(0)
    middle()
    relay(1, near)
    backs(0, 0)
    backs(0, 1)
    columns(1, core)
    send_sums(0, 0)
    complete(1)
    columns(1, 1 - core)
    send_sums(0, 1)
    fronts(1)
    middle()
    backs(1, 0)
    backs(1, 1)
    rows(2)
    send_sums(1, 0)
    rows(3)
    send_sums(1, 1)
    rows(4)

    def wait_pen():
        for d in range(1, peers):
            src = down(d)
            when(
                active(src),
                lambda: remote(
                    pen_send.at[0, 0], pen_recv.at[src], p_send_sem.at[d], p_recv_sem.at[d], (e, c, r)
                ).wait_recv(),
            )
        held = pen_recv[...].astype(F32).reshape(rb, 2 * s_local, zp)
        flat[...] = flat[...] - jnp.concatenate([held[:, k, :nz] for k in range(2 * s_local)], axis=1)

    def hops(s):
        for d in range(1, chips):
            src = lax.rem(chip + chips - d, chips)
            remote(
                rs_send.at[s, src], rs_recv.at[s, src], rs_send_sem.at[s, d], rs_recv_sem.at[s, d], (e, partner, r)
            ).wait_recv()

    def finish(s):
        mine, slot = chip // group, lax.rem(chip, group)
        total = part[s, mine, slot, core].astype(F32) + paired[s, mine, slot].astype(F32)
        for d in range(1, chips):
            total = total + rs_recv[s, lax.rem(chip + chips - d, chips)].astype(F32)
        at = slice(s * width, (s + 1) * width)
        out_ref[:, at] = flat[:, at] - dc_ref[0] * total

    wait_pen()
    for s in range(s_local):
        hops(s)
        finish(s)

    for s in range(s_local):
        gather(s, None).wait_send()
        for d in range(1, chips):
            gather(s, d).wait_send()
            forward(s, d).wait_send()
            scatter(s, lax.rem(chip + d, chips)).wait_send()
    for s in range(s_local):
        for j in range(2):
            pair(s, j).wait_send()
    for d in range(1, peers):
        when(active(up(d)), lambda: window(d).wait_send())
        when(active(q), lambda: penalty_out(d).wait_send())
    pl.when(c < n_c - 1)(lambda: edge_up().wait_send())
    pl.when(c > 0)(lambda: edge_down().wait_send())


def body(kspace, sampling, coil_maps, image, filters, thresholds, dc_weight):
    n_e, n_c, n_r = lax.axis_size("echo"), lax.axis_size("coil"), lax.axis_size("read")
    rb, _, s_local, _, nz = image.shape
    ny = kspace.shape[0]
    peers = n_e * n_r
    rq = window_rows(rb, peers)
    n_q = rb // rq
    zp = -(-(nz + 1) // 128) * 128
    width = 2 * nz
    slices = s_local * n_r
    taps = 2 * slices
    count = filters.shape[0]

    col_cos, col_sin = tables(nz)
    row_cos, row_sin = tables(ny)
    gap = ((0, zp - nz), (0, zp - nz))
    col_cos, col_sin = np.pad(col_cos, gap), np.pad(col_sin, gap)
    fz = jnp.asarray(np.block([[col_cos, -col_sin], [col_sin, col_cos]]), BF16)
    az = jnp.asarray(np.block([[col_cos, col_sin], [-col_sin, col_cos]]), BF16)
    ty = jnp.asarray(np.concatenate([row_cos, row_sin], 1), BF16)

    spread = np.zeros((slices, 3, SLAB, 3, 3, 3, 2))
    for at in range(slices):
        for a in range(3):
            for b in range(3):
                for d in range(3):
                    for p in range(2):
                        if 0 <= at + b - 1 < slices:
                            spread[at, a, d * taps + (at + b - 1) * 2 + p, a, b, d, p] = 1.0
    spread = jnp.asarray(spread.reshape(slices, 3 * SLAB, 54), BF16)

    k_view = jnp.transpose(kspace[:, 0, 0], (1, 2, 3, 0))
    m_view = jnp.transpose(coil_maps[:, 0], (1, 2, 3, 0))
    s_view = jnp.transpose(sampling[:, 0], (1, 0))

    operands = tuple(
        pltpu.with_memory_space_constraint(x, pltpu.HBM)
        for x in (
            image[:, 0], spread, jnp.transpose(filters, (1, 2, 3, 4, 0)), thresholds[None, :],
            k_view, m_view, s_view, fz, az, ty,
        )
    )
    vmem = pl.BlockSpec(memory_space=pltpu.VMEM)
    hbm = pl.BlockSpec(memory_space=pltpu.HBM)
    smem = pl.BlockSpec(memory_space=pltpu.SMEM)
    dma = pltpu.SemaphoreType.DMA
    updated = pl.pallas_call(
        functools.partial(kernel, (n_e, n_c, n_r, n_q, rq, nz, ny)),
        out_shape=jax.ShapeDtypeStruct((rb, s_local * width), F32),
        in_specs=[hbm] * 4 + [smem] + [hbm] * 6,
        out_specs=vmem,
        scratch_shapes=[
            pltpu.VMEM((rb, s_local, 2, nz), F32),
            pltpu.VMEM((rb, s_local * width), F32),
            pltpu.VMEM((rb + 2 * (rq + 2), 2 * s_local, zp), BF16),
            pltpu.VMEM(spread.shape, BF16),
            pltpu.VMEM((3, 3, 3, 2, count), BF16),
            pltpu.VMEM((1, count), F32),
            pltpu.VMEM((s_local, n_c, rb, width), BF16),
            pltpu.VMEM((s_local, 2, n_c // 4, 2, rb, width), BF16),
            pltpu.VMEM((s_local, 2, n_c // 4, rb, width), BF16),
            pltpu.VMEM((s_local, n_c // 2, rb, width), BF16),
            pltpu.VMEM((s_local, n_c // 2, rb, width), BF16),
            pltpu.VMEM((3 * SLAB, slices * count), BF16),
            pltpu.VMEM((slices * count, 3 * SLAB), BF16),
            pltpu.VMEM((slices * count, zp), F32),
            pltpu.VMEM((n_e, n_r, rq + 4, 2 * s_local, zp), BF16),
            pltpu.VMEM((2, n_e, n_r, 2, 2 * s_local, zp), BF16),
            pltpu.VMEM((n_e, n_r, rq, 2 * s_local, zp), BF16),
            pltpu.VMEM((n_q, rq, 2 * s_local, zp), BF16),
            pltpu.VMEM((n_e, rq + 4, SLAB, zp), F32),
            pltpu.VMEM((n_e, (rq + 4) * SLAB, zp), BF16),
            pltpu.VMEM(k_view.shape, BF16),
            pltpu.VMEM(m_view.shape, BF16),
            pltpu.VMEM(s_view.shape, jnp.int32),
            pltpu.VMEM(fz.shape, BF16),
            pltpu.VMEM(az.shape, BF16),
            pltpu.VMEM(ty.shape, BF16),
            pltpu.VMEM((s_local, ny, 2 * zp), BF16),
            pltpu.VMEM((s_local, ny, 2 * zp), BF16),
            pltpu.VMEM((ny, zp), F32),
            pltpu.VMEM((ny, 2 * zp), BF16),
            pltpu.VMEM((2 * ny, 2 * zp), BF16),
            dma((10,)),
            dma((s_local, n_c)), dma((s_local, n_c)),
            dma((peers,)), dma((peers,)),
            dma((2,)), dma((2, peers)),
            dma((peers,)), dma((peers,)),
            dma((s_local, n_c)), dma((s_local, n_c)),
            dma((s_local, n_c)), dma((s_local, n_c)), dma((s_local, 2)), dma((s_local, 2)),
        ],
        compiler_params=pltpu.CompilerParams(
            collective_id=0, has_side_effects=True, vmem_limit_bytes=GRANT
        ),
        name="cascade",
    )(*operands[:4], dc_weight, *operands[4:])
    return updated.reshape(image.shape)


def solution(mesh):
    return jax.shard_map(
        body,
        mesh=mesh,
        in_specs=(
            P(None, "echo", "coil", "read", None, None),
            P(None, "echo", None),
            P(None, "coil", "read", None, None),
            P("coil", "echo", "read", None, None),
            P(),
            P(),
            P("echo"),
        ),
        out_specs=P("coil", "echo", "read", None, None),
        check_vma=False,
    )
```

```python
import functools
import math

import numpy as np
import jax
import jax.numpy as jnp
from jax import lax
from jax.experimental import pallas as pl
from jax.experimental.pallas import tpu as pltpu
from jax.sharding import PartitionSpec as P

MESH = pl.DeviceIdType.MESH
F32 = jnp.float32
BF16 = jnp.bfloat16
SLAB = 32
GRANT = 24 << 20
TINY = float(np.finfo(np.float32).tiny)
SPLITS = (7, 7, 11, 11)


def tables(length):
    product = np.outer(np.arange(length), np.arange(length)) % length
    phases = product * (2.0 * np.pi / length)
    normalize = length ** (-0.5)
    return np.cos(phases) * normalize, np.sin(phases) * normalize


def window_rows(rows, peers):
    for size in range(2, rows + 1):
        if rows % size == 0 and rows // size <= peers:
            return size
    return rows


def dot(left, right):
    return jnp.dot(left, right, preferred_element_type=F32)


def kernel(
    cfg,
    image_hbm, spread_hbm, filters_hbm, thr_hbm, dc_ref, kspace_hbm, maps_hbm, samp_hbm, fz_hbm, az_hbm, ty_hbm,
    out_ref,
    image, flat, padded, spread, filters, thr,
    gat, part, paired, rs_send, rs_recv, wide_ref, tall_ref, level, ext, edge, pen_send, pen_recv, pacc, slab,
    kspace, maps, samp, fz, az, ty, k_rows, m_rows, s_rows, weighted, stack,
    local_sem, ag_send_sem, ag_recv_sem, x_send_sem, x_recv_sem, e_send_sem, e_recv_sem,
    p_send_sem, p_recv_sem, rs_send_sem, rs_recv_sem, f_send_sem, f_recv_sem, pair_send_sem, pair_recv_sem,
):
    n_e, n_c, n_r, n_q, rq, nz, ny = cfg
    peers = n_e * n_r
    e = lax.axis_index("echo")
    c = lax.axis_index("coil")
    r = lax.axis_index("read")
    q = e * n_r + r
    s_local, rb = rs_send.shape[0], flat.shape[0]
    chips = n_c // 2
    core = lax.rem(c, 2)
    chip = c // 2
    partner = c + 1 - 2 * core
    width = 2 * nz
    zp = ext.shape[-1]
    half = ny // 2
    group = chips // 2
    side = jnp.where(chip < group, 1, 0)

    loads = [
        pltpu.make_async_copy(src, dst, local_sem.at[i])
        for i, (src, dst) in enumerate(
            [
                (image_hbm, image), (spread_hbm, spread), (filters_hbm, filters), (thr_hbm, thr),
                (maps_hbm, maps), (fz_hbm, fz), (ty_hbm, ty), (kspace_hbm, kspace), (samp_hbm, samp), (az_hbm, az),
            ]
        )
    ]

    for load in loads:
        load.start()

    def remote(src, dst, send, recv, target):
        return pltpu.make_async_remote_copy(
            src_ref=src, dst_ref=dst, send_sem=send, recv_sem=recv, device_id=target, device_id_type=MESH
        )

    def when(condition, act):
        if condition is True:
            act()
        else:
            pl.when(condition)(act)

    def up(d):
        return lax.rem(q + d, peers)

    def down(d):
        return lax.rem(q + peers - d, peers)

    def active(which):
        return True if n_q == peers else which < n_q

    barrier = pltpu.get_barrier_semaphore()
    for d in range(chips):
        to = lax.rem(c + 2 * d, n_c) if d else partner
        pl.semaphore_signal(barrier, inc=1, device_id=(e, to, r), device_id_type=MESH)
    for d in range(peers):
        if d:
            pl.semaphore_signal(barrier, inc=1, device_id=(up(d) // n_r, c, lax.rem(up(d), n_r)), device_id_type=MESH)
        for step, ok in ((1, c < n_c - 1), (-1, c > 0)):
            @pl.when(ok)
            def _():
                pl.semaphore_signal(
                    barrier, inc=1, device_id=(up(d) // n_r, c + step, lax.rem(up(d), n_r)), device_id_type=MESH
                )
    margin = rq + 2
    padded[...] = jnp.zeros_like(padded)
    loads[0].wait()
    flat[...] = jnp.concatenate([image[:, s, p, :] for s in range(s_local) for p in range(2)], axis=1)
    for s in range(s_local):
        gat[s, c] = flat[:, s * width : (s + 1) * width].astype(BF16)

    padded[margin : margin + rb, :, :nz] = image[...].reshape(rb, 2 * s_local, nz).astype(BF16)
    sides = jnp.minimum(c, 1) + jnp.minimum(n_c - 1 - c, 1)
    pl.semaphore_wait(barrier, chips + peers - 1 + peers * sides)

    def window(d):
        to = up(d)
        return remote(
            padded.at[pl.ds((1 + to) * rq, rq + 4)], ext.at[e, r], x_send_sem.at[d], x_recv_sem.at[d], (to // n_r, c, lax.rem(to, n_r))
        )

    last = n_q - 1
    def edge_up():
        return remote(
            padded.at[pl.ds(margin + rb - 2, 2)], edge.at[0, e, r], e_send_sem.at[0], e_recv_sem.at[0, q], (0, c + 1, 0)
        )

    def edge_down():
        return remote(
            padded.at[pl.ds(margin, 2)], edge.at[1, e, r], e_send_sem.at[1], e_recv_sem.at[1, q],
            (last // n_r, c - 1, last % n_r),
        )

    def gather(s, d):
        to = lax.rem(c + 2 * d, n_c) if d is not None else partner
        at = 0 if d is None else d
        return remote(gat.at[s, c], gat.at[s, c], ag_send_sem.at[s, at], ag_recv_sem.at[s, at], (e, to, r))

    def gathered(s, d):
        src = lax.rem(c + n_c - 2 * d, n_c)
        return remote(gat.at[s, src], gat.at[s, src], ag_send_sem.at[s, d], ag_recv_sem.at[s, d], (e, partner, r))

    def forward(s, d):
        src = lax.rem(c + n_c - 2 * d, n_c)
        return remote(gat.at[s, src], gat.at[s, src], f_send_sem.at[s, d], f_recv_sem.at[s, d], (e, partner, r))

    def targets(act, dists):
        for dist in dists:
            pl.when(chip + dist < chips)(lambda: act(dist))
            pl.when(chip - dist >= 0)(lambda: act(chips - dist))

    def relay(s, dists):
        def one(d):
            gathered(s, d).wait_recv()
            forward(s, d).start()

        for dist in dists:
            pl.when(chip - dist >= 0)(lambda: one(dist))
            pl.when(chip + dist < chips)(lambda: one(chips - dist))

    near = range(1, chips)
    far = near[::-1]

    for d in range(1, peers):
        when(active(up(d)), lambda: window(d).start())
    pl.when(c < n_c - 1)(lambda: edge_up().start())
    pl.when(c > 0)(lambda: edge_down().start())
    for s in range(s_local):
        targets(lambda d: gather(s, d).start(), near if s else far)
        gather(s, None).start()

    def complete(s):
        remote(
            gat.at[s, partner], gat.at[s, partner], ag_send_sem.at[s, 0], ag_recv_sem.at[s, 0], (e, partner, r)
        ).wait_recv()
        for d in range(1, chips):
            src = lax.rem(partner + n_c - 2 * d, n_c)
            remote(
                gat.at[s, src], gat.at[s, src], f_send_sem.at[s, d], f_recv_sem.at[s, d], (e, partner, r)
            ).wait_recv()

    count = filters.shape[-1]
    slices = s_local * n_r
    band = pen_send.shape[3]
    for load in loads[1:4]:
        load.wait()
    flat_filters = filters[...].astype(F32).reshape(-1, count).astype(BF16)
    pieces = [dot(spread[at], flat_filters) for at in range(slices)]
    for at in range(slices):
        wide_ref[:, at * count : (at + 1) * count] = pieces[at].astype(BF16)
        tall_ref[at * count : (at + 1) * count, :] = pieces[at].T.astype(BF16)
    shape = (slices, count, count)
    on = lax.broadcasted_iota(jnp.int32, shape, 1) == lax.broadcasted_iota(jnp.int32, shape, 2)
    column = jnp.sum(jnp.where(on, thr[...].reshape(1, 1, count), 0.0), axis=2, keepdims=True)
    level[...] = jnp.broadcast_to(column, (slices, count, zp)).reshape(slices * count, zp)

    def prepare():
        ext[e, r] = padded[pl.ds((1 + q) * rq, rq + 4)]
        for d in range(1, peers):
            src = down(d)
            remote(
                padded.at[pl.ds(0, rq + 4)], ext.at[src // n_r, lax.rem(src, n_r)], x_send_sem.at[d], x_recv_sem.at[d], (e, c, r)
            ).wait_recv()

        def border(which, begin):
            for src in range(peers):
                at = (which, src // n_r, src % n_r)
                remote(
                    padded.at[pl.ds(0, 2)], edge.at[at], e_send_sem.at[0], e_recv_sem.at[which, src], (e, c, r)
                ).wait_recv()
                ext[src // n_r, src % n_r, begin : begin + 2] = edge[at]

        pl.when(jnp.logical_and(q == 0, c > 0))(lambda: border(0, 0))
        pl.when(jnp.logical_and(q == last, c < n_c - 1))(lambda: border(1, rq + 2))

        rows = rq + 4
        taps = 2 * s_local * n_r
        for echo in range(n_e):
            parts = [ext[echo, read].astype(F32) for read in range(n_r)]
            block = jnp.concatenate(parts, axis=1) if n_r > 1 else parts[0]
            flat = block.reshape(rows * taps, zp)
            moved = [
                pltpu.roll(flat, 1, 1).reshape(rows, taps, zp),
                block,
                pltpu.roll(flat, zp - 1, 1).reshape(rows, taps, zp),
            ]
            fill = [jnp.zeros((rows, SLAB - 3 * taps, zp), F32)] if SLAB > 3 * taps else []
            slab[echo] = jnp.concatenate(moved + fill, axis=1).reshape(rows * SLAB, zp).astype(BF16)

        pacc[...] = jnp.zeros_like(pacc)

    def respond(begin, end):
        tall = tall_ref[...]
        wide = wide_ref[...]
        first = c * rb + q * rq - 1

        for i in range(begin, end):
            window = slice(i * SLAB, (i + 3) * SLAB)
            response = [dot(tall, slab[echo, window, :]) for echo in range(n_e)]
            energy = response[0] * response[0]
            for other in response[1:]:
                energy = energy + other * other
            factor = 1.0 / (1.0 + level[...] * lax.rsqrt(jnp.maximum(energy, TINY)))
            if i in (0, rq + 1):
                inside = jnp.logical_and(first + i >= 0, first + i < ny)
                factor = jnp.where(inside, factor, 0.0)
            for echo in range(n_e):
                spread = dot(wide, (response[echo] * factor).astype(BF16))
                for a in range(3):
                    pacc[echo, i + a] += spread[a * SLAB : (a + 1) * SLAB]

    def collect():
        taps = 2 * s_local * n_r
        lane = lax.broadcasted_iota(jnp.int32, (1, 1, zp), 2)
        for echo in range(n_e):
            held = pacc[echo, 2 : 2 + rq]
            low = pltpu.roll(held[:, :taps].reshape(rq * taps, zp), zp - 1, 1).reshape(rq, taps, zp)
            high = pltpu.roll(held[:, 2 * taps : 3 * taps].reshape(rq * taps, zp), 1, 1).reshape(rq, taps, zp)
            low = jnp.where(lane < nz - 1, low, 0.0)
            high = jnp.where(lane > 0, high, 0.0)
            total = low + held[:, taps : 2 * taps] + high
            for read in range(n_r):
                own = range(read * 2 * s_local, (read + 1) * 2 * s_local)
                dense = jnp.concatenate([total[:, k, :nz] for k in own], axis=1)
                for k in range(rq // band):
                    pen_send[echo, read, k] = dense[k * band : (k + 1) * band]
        pen_recv[q] = pen_send[e, r]

    def penalty_out(d):
        to = up(d)
        return remote(
            pen_send.at[to // n_r, lax.rem(to, n_r)], pen_recv.at[q], p_send_sem.at[d], p_recv_sem.at[d],
            (to // n_r, c, lax.rem(to, n_r)),
        )

    marks = [0] + [(rq + 2) * part // 14 for part in SPLITS] + [rq + 2]

    def rows(at):
        def act():
            if at == 0:
                prepare()
            respond(marks[at], marks[at + 1])
            if at == len(marks) - 2:
                collect()
                for d in range(1, peers):
                    penalty_out(d).start()

        when(active(q), act)

    def turn():
        for load in loads[4:]:
            load.wait()
        for buf in (k_rows, m_rows, weighted):
            buf[...] = jnp.zeros_like(buf)
        for s in range(s_local):
            for p in range(2):
                at = slice(p * zp, p * zp + nz)
                k_rows[s, :, at] = kspace[s, p].astype(F32).T.astype(BF16)
                m_rows[s, :, at] = maps[s, p].astype(F32).T.astype(BF16)
        s_rows[:, :nz] = samp[...].astype(F32).T
        s_rows[:, nz:] = jnp.zeros((ny, zp - nz), F32)

    def halves(j):
        return side if j == 0 else 1 - side

    def pair(s, j):
        h = halves(j)
        return remote(
            part.at[s, h, :, 1 - core], paired.at[s, h], pair_send_sem.at[s, j], pair_recv_sem.at[s, j],
            (e, partner, r),
        )

    def scatter(s, to):
        d = lax.rem(to - chip + chips, chips)
        return remote(
            rs_send.at[s, to], rs_recv.at[s, chip], rs_send_sem.at[s, d], rs_recv_sem.at[s, d],
            (e, 2 * to + core, r),
        )

    def send_sums(s, j):
        pair(s, j).wait_recv()
        h = halves(j)
        sums = (part[s, h, :, core].astype(F32) + paired[s, h].astype(F32)).astype(BF16)
        for k in range(group):
            to = h * group + k
            rs_send[s, to] = sums[k]
            if j:
                pl.when(to != chip)(lambda: scatter(s, to).start())
            else:
                scatter(s, to).start()

    def swapped(x, sign):
        low, high = x[:, :zp], x[:, zp:]
        return jnp.concatenate([high, -low] if sign > 0 else [-high, low], axis=1)

    def columns(s, which):
        starts = [pl.multiple_of((2 * k + which) * rb, 8) for k in range(chips)]
        image = jnp.concatenate([gat[s, 2 * k + which] for k in range(chips)], axis=0)
        sense = jnp.concatenate([m_rows[s, pl.ds(at, rb), :] for at in starts], axis=0)
        real, imag = image[:, :nz].astype(F32), image[:, nz:].astype(F32)
        map_real, map_imag = sense[:, :nz].astype(F32), sense[:, zp : zp + nz].astype(F32)
        weighted[:half, :nz] = (map_real * real - map_imag * imag).astype(BF16)
        weighted[:half, zp : zp + nz] = (map_real * imag + map_imag * real).astype(BF16)
        halfway = dot(weighted[:half, :], fz[...])
        upper, lower = halfway.astype(BF16), swapped(halfway, 1).astype(BF16)
        for k, at in enumerate(starts):
            stack[pl.ds(at, rb), :] = upper[k * rb : (k + 1) * rb]
            stack[pl.ds(ny + at, rb), :] = lower[k * rb : (k + 1) * rb]

    def fronts(s):
        spectrum = dot(ty[...], stack[...])
        sampled = s_rows[...]
        sampled = jnp.concatenate([sampled, sampled], axis=1)
        residual = sampled * (spectrum - k_rows[s].astype(F32))
        stack[:ny] = residual.astype(BF16)
        stack[ny:] = swapped(residual, -1).astype(BF16)

    def middle():
        weighted[...] = dot(ty[...], stack[...]).astype(BF16)

    def backs(s, j):
        h = halves(j)
        at = pl.ds(pl.multiple_of(h * half, 16), half)
        restored = dot(weighted[at, :], az[...])
        back_real, back_imag = restored[:, :nz], restored[:, zp : zp + nz]
        map_real, map_imag = m_rows[s, at, :nz].astype(F32), m_rows[s, at, zp : zp + nz].astype(F32)
        adjoint = jnp.concatenate(
            [
                (map_real * back_real + map_imag * back_imag).astype(BF16),
                (map_real * back_imag - map_imag * back_real).astype(BF16),
            ],
            axis=1,
        )
        part[s, h] = adjoint.reshape(group, 2, rb, width)
        pair(s, j).start()

    turn()
    rows(0)
    relay(0, near)
    columns(0, core)
    complete(0)
    columns(0, 1 - core)
    fronts(0)
    middle()
    backs(0, 0)
    relay(1, near)
    backs(0, 1)
    columns(1, core)
    rows(1)
    send_sums(0, 0)
    complete(1)
    columns(1, 1 - core)
    send_sums(0, 1)
    fronts(1)
    middle()
    backs(1, 0)
    backs(1, 1)
    rows(2)
    send_sums(1, 0)
    rows(3)
    send_sums(1, 1)
    rows(4)

    def wait_pen():
        for d in range(1, peers):
            src = down(d)
            when(
                active(src),
                lambda: remote(
                    pen_send.at[0, 0], pen_recv.at[src], p_send_sem.at[d], p_recv_sem.at[d], (e, c, r)
                ).wait_recv(),
            )
        for at in range(n_q):
            for k in range(rq // band):
                row = at * rq + k * band
                flat[row : row + band, :] = flat[row : row + band, :] - pen_recv[at, k]

    def hops(s):
        for d in range(1, chips):
            src = lax.rem(chip + chips - d, chips)
            remote(
                rs_send.at[s, src], rs_recv.at[s, src], rs_send_sem.at[s, d], rs_recv_sem.at[s, d], (e, partner, r)
            ).wait_recv()

    def finish(s):
        mine, slot = chip // group, lax.rem(chip, group)
        total = part[s, mine, slot, core].astype(F32) + paired[s, mine, slot].astype(F32)
        for d in range(1, chips):
            total = total + rs_recv[s, lax.rem(chip + chips - d, chips)].astype(F32)
        at = slice(s * width, (s + 1) * width)
        out_ref[:, at] = flat[:, at] - dc_ref[0] * total

    wait_pen()
    for s in range(s_local):
        hops(s)
        finish(s)

    for s in range(s_local):
        gather(s, None).wait_send()
        for d in range(1, chips):
            gather(s, d).wait_send()
            forward(s, d).wait_send()
            scatter(s, lax.rem(chip + d, chips)).wait_send()
    for s in range(s_local):
        for j in range(2):
            pair(s, j).wait_send()
    for d in range(1, peers):
        when(active(up(d)), lambda: window(d).wait_send())
        when(active(q), lambda: penalty_out(d).wait_send())
    pl.when(c < n_c - 1)(lambda: edge_up().wait_send())
    pl.when(c > 0)(lambda: edge_down().wait_send())


def body(kspace, sampling, coil_maps, image, filters, thresholds, dc_weight):
    n_e, n_c, n_r = lax.axis_size("echo"), lax.axis_size("coil"), lax.axis_size("read")
    rb, _, s_local, _, nz = image.shape
    ny = kspace.shape[0]
    peers = n_e * n_r
    rq = window_rows(rb, peers)
    n_q = rb // rq
    zp = -(-(nz + 1) // 128) * 128
    width = 2 * nz
    slices = s_local * n_r
    taps = 2 * slices
    band = math.gcd(rq, 4)
    count = filters.shape[0]

    col_cos, col_sin = tables(nz)
    row_cos, row_sin = tables(ny)
    gap = ((0, zp - nz), (0, zp - nz))
    col_cos, col_sin = np.pad(col_cos, gap), np.pad(col_sin, gap)
    fz = jnp.asarray(np.block([[col_cos, -col_sin], [col_sin, col_cos]]), BF16)
    az = jnp.asarray(np.block([[col_cos, col_sin], [-col_sin, col_cos]]), BF16)
    ty = jnp.asarray(np.concatenate([row_cos, row_sin], 1), BF16)

    spread = np.zeros((slices, 3, SLAB, 3, 3, 3, 2))
    for at in range(slices):
        for a in range(3):
            for b in range(3):
                for d in range(3):
                    for p in range(2):
                        if 0 <= at + b - 1 < slices:
                            spread[at, a, d * taps + (at + b - 1) * 2 + p, a, b, d, p] = 1.0
    spread = jnp.asarray(spread.reshape(slices, 3 * SLAB, 54), BF16)

    k_view = jnp.transpose(kspace[:, 0, 0], (1, 2, 3, 0))
    m_view = jnp.transpose(coil_maps[:, 0], (1, 2, 3, 0))
    s_view = jnp.transpose(sampling[:, 0], (1, 0))

    operands = tuple(
        pltpu.with_memory_space_constraint(x, pltpu.HBM)
        for x in (
            image[:, 0], spread, jnp.transpose(filters, (1, 2, 3, 4, 0)), thresholds[None, :],
            k_view, m_view, s_view, fz, az, ty,
        )
    )
    vmem = pl.BlockSpec(memory_space=pltpu.VMEM)
    hbm = pl.BlockSpec(memory_space=pltpu.HBM)
    smem = pl.BlockSpec(memory_space=pltpu.SMEM)
    dma = pltpu.SemaphoreType.DMA
    updated = pl.pallas_call(
        functools.partial(kernel, (n_e, n_c, n_r, n_q, rq, nz, ny)),
        out_shape=jax.ShapeDtypeStruct((rb, s_local * width), F32),
        in_specs=[hbm] * 4 + [smem] + [hbm] * 6,
        out_specs=vmem,
        scratch_shapes=[
            pltpu.VMEM((rb, s_local, 2, nz), F32),
            pltpu.VMEM((rb, s_local * width), F32),
            pltpu.VMEM((rb + 2 * (rq + 2), 2 * s_local, zp), BF16),
            pltpu.VMEM(spread.shape, BF16),
            pltpu.VMEM((3, 3, 3, 2, count), BF16),
            pltpu.VMEM((1, count), F32),
            pltpu.VMEM((s_local, n_c, rb, width), BF16),
            pltpu.VMEM((s_local, 2, n_c // 4, 2, rb, width), BF16),
            pltpu.VMEM((s_local, 2, n_c // 4, rb, width), BF16),
            pltpu.VMEM((s_local, n_c // 2, rb, width), BF16),
            pltpu.VMEM((s_local, n_c // 2, rb, width), BF16),
            pltpu.VMEM((3 * SLAB, slices * count), BF16),
            pltpu.VMEM((slices * count, 3 * SLAB), BF16),
            pltpu.VMEM((slices * count, zp), F32),
            pltpu.VMEM((n_e, n_r, rq + 4, 2 * s_local, zp), BF16),
            pltpu.VMEM((2, n_e, n_r, 2, 2 * s_local, zp), BF16),
            pltpu.VMEM((n_e, n_r, rq // band, band, s_local * width), F32),
            pltpu.VMEM((n_q, rq // band, band, s_local * width), F32),
            pltpu.VMEM((n_e, rq + 4, SLAB, zp), F32),
            pltpu.VMEM((n_e, (rq + 4) * SLAB, zp), BF16),
            pltpu.VMEM(k_view.shape, BF16),
            pltpu.VMEM(m_view.shape, BF16),
            pltpu.VMEM(s_view.shape, jnp.int32),
            pltpu.VMEM(fz.shape, BF16),
            pltpu.VMEM(az.shape, BF16),
            pltpu.VMEM(ty.shape, BF16),
            pltpu.VMEM((s_local, ny, 2 * zp), BF16),
            pltpu.VMEM((s_local, ny, 2 * zp), BF16),
            pltpu.VMEM((ny, zp), F32),
            pltpu.VMEM((ny, 2 * zp), BF16),
            pltpu.VMEM((2 * ny, 2 * zp), BF16),
            dma((10,)),
            dma((s_local, n_c)), dma((s_local, n_c)),
            dma((peers,)), dma((peers,)),
            dma((2,)), dma((2, peers)),
            dma((peers,)), dma((peers,)),
            dma((s_local, n_c)), dma((s_local, n_c)),
            dma((s_local, n_c)), dma((s_local, n_c)), dma((s_local, 2)), dma((s_local, 2)),
        ],
        compiler_params=pltpu.CompilerParams(
            collective_id=0, has_side_effects=True, vmem_limit_bytes=GRANT
        ),
        name="cascade",
    )(*operands[:4], dc_weight, *operands[4:])
    return updated.reshape(image.shape)


def solution(mesh):
    return jax.shard_map(
        body,
        mesh=mesh,
        in_specs=(
            P(None, "echo", "coil", "read", None, None),
            P(None, "echo", None),
            P(None, "coil", "read", None, None),
            P("coil", "echo", "read", None, None),
            P(),
            P(),
            P("echo"),
        ),
        out_specs=P("coil", "echo", "read", None, None),
        check_vma=False,
    )
```

```python
import functools
import math

import numpy as np
import jax
import jax.numpy as jnp
from jax import lax
from jax.experimental import pallas as pl
from jax.experimental.pallas import tpu as pltpu
from jax.sharding import PartitionSpec as P

MESH = pl.DeviceIdType.MESH
F32 = jnp.float32
BF16 = jnp.bfloat16
SLAB = 32
GRANT = 24 << 20
TINY = float(np.finfo(np.float32).tiny)
SPLITS = (7, 7, 11, 11)


def tables(length):
    product = np.outer(np.arange(length), np.arange(length)) % length
    phases = product * (2.0 * np.pi / length)
    normalize = length ** (-0.5)
    return np.cos(phases) * normalize, np.sin(phases) * normalize


def window_rows(rows, peers):
    for size in range(2, rows + 1):
        if rows % size == 0 and rows // size <= peers:
            return size
    return rows


def dot(left, right):
    return jnp.dot(left, right, preferred_element_type=F32)


def kernel(
    cfg,
    image_hbm, spread_hbm, filters_hbm, thr_hbm, dc_ref, kspace_hbm, maps_hbm, samp_hbm, fz_hbm, az_hbm, ty_hbm,
    out_ref,
    image, flat, padded, spread, filters, thr,
    gat, part, paired, rs_send, rs_recv, wide_ref, tall_ref, level, ext, edge, pen_send, pen_recv, pacc, slab,
    kspace, maps, samp, fz, az, ty, k_rows, m_rows, s_rows, weighted, stack,
    local_sem, ag_send_sem, ag_recv_sem, x_send_sem, x_recv_sem, e_send_sem, e_recv_sem,
    p_send_sem, p_recv_sem, rs_send_sem, rs_recv_sem, f_send_sem, f_recv_sem, pair_send_sem, pair_recv_sem,
):
    n_e, n_c, n_r, n_q, rq, nz, ny = cfg
    peers = n_e * n_r
    e = lax.axis_index("echo")
    c = lax.axis_index("coil")
    r = lax.axis_index("read")
    q = e * n_r + r
    s_local, rb = rs_send.shape[0], flat.shape[0]
    chips = n_c // 2
    core = lax.rem(c, 2)
    chip = c // 2
    partner = c + 1 - 2 * core
    width = 2 * nz
    zp = ext.shape[-1]
    half = ny // 2
    group = chips // 2
    side = jnp.where(chip < group, 1, 0)

    loads = [
        pltpu.make_async_copy(src, dst, local_sem.at[i])
        for i, (src, dst) in enumerate(
            [
                (image_hbm, image), (spread_hbm, spread), (filters_hbm, filters), (thr_hbm, thr),
                (maps_hbm, maps), (fz_hbm, fz), (ty_hbm, ty), (kspace_hbm, kspace), (samp_hbm, samp), (az_hbm, az),
            ]
        )
    ]

    for load in loads:
        load.start()

    def remote(src, dst, send, recv, target):
        return pltpu.make_async_remote_copy(
            src_ref=src, dst_ref=dst, send_sem=send, recv_sem=recv, device_id=target, device_id_type=MESH
        )

    def when(condition, act):
        if condition is True:
            act()
        else:
            pl.when(condition)(act)

    def up(d):
        return lax.rem(q + d, peers)

    def down(d):
        return lax.rem(q + peers - d, peers)

    def active(which):
        return True if n_q == peers else which < n_q

    barrier = pltpu.get_barrier_semaphore()
    for d in range(chips):
        to = lax.rem(c + 2 * d, n_c) if d else partner
        pl.semaphore_signal(barrier, inc=1, device_id=(e, to, r), device_id_type=MESH)
    for d in range(peers):
        if d:
            pl.semaphore_signal(barrier, inc=1, device_id=(up(d) // n_r, c, lax.rem(up(d), n_r)), device_id_type=MESH)
        for step, ok in ((1, c < n_c - 1), (-1, c > 0)):
            @pl.when(ok)
            def _():
                pl.semaphore_signal(
                    barrier, inc=1, device_id=(up(d) // n_r, c + step, lax.rem(up(d), n_r)), device_id_type=MESH
                )
    margin = rq + 2
    padded[...] = jnp.zeros_like(padded)
    loads[0].wait()
    flat[...] = jnp.concatenate([image[:, s, p, :] for s in range(s_local) for p in range(2)], axis=1)
    for s in range(s_local):
        gat[s, c] = flat[:, s * width : (s + 1) * width].astype(BF16)

    padded[margin : margin + rb, :, :nz] = image[...].reshape(rb, 2 * s_local, nz).astype(BF16)
    sides = jnp.minimum(c, 1) + jnp.minimum(n_c - 1 - c, 1)
    pl.semaphore_wait(barrier, chips + peers - 1 + peers * sides)

    def window(d):
        to = up(d)
        return remote(
            padded.at[pl.ds((1 + to) * rq, rq + 4)], ext.at[e, r], x_send_sem.at[d], x_recv_sem.at[d], (to // n_r, c, lax.rem(to, n_r))
        )

    last = n_q - 1
    def edge_up():
        return remote(
            padded.at[pl.ds(margin + rb - 2, 2)], edge.at[0, e, r], e_send_sem.at[0], e_recv_sem.at[0, q], (0, c + 1, 0)
        )

    def edge_down():
        return remote(
            padded.at[pl.ds(margin, 2)], edge.at[1, e, r], e_send_sem.at[1], e_recv_sem.at[1, q],
            (last // n_r, c - 1, last % n_r),
        )

    def gather(s, d):
        to = lax.rem(c + 2 * d, n_c) if d is not None else partner
        at = 0 if d is None else d
        return remote(gat.at[s, c], gat.at[s, c], ag_send_sem.at[s, at], ag_recv_sem.at[s, at], (e, to, r))

    def gathered(s, d):
        src = lax.rem(c + n_c - 2 * d, n_c)
        return remote(gat.at[s, src], gat.at[s, src], ag_send_sem.at[s, d], ag_recv_sem.at[s, d], (e, partner, r))

    def forward(s, d):
        src = lax.rem(c + n_c - 2 * d, n_c)
        return remote(gat.at[s, src], gat.at[s, src], f_send_sem.at[s, d], f_recv_sem.at[s, d], (e, partner, r))

    def targets(act, dists):
        for dist in dists:
            pl.when(chip + dist < chips)(lambda: act(dist))
            pl.when(chip - dist >= 0)(lambda: act(chips - dist))

    def relay(s, dists):
        def one(d):
            gathered(s, d).wait_recv()
            forward(s, d).start()

        for dist in dists:
            pl.when(chip - dist >= 0)(lambda: one(dist))
            pl.when(chip + dist < chips)(lambda: one(chips - dist))

    near = range(1, chips)
    far = near[::-1]

    pl.when(c < n_c - 1)(lambda: edge_up().start())
    pl.when(c > 0)(lambda: edge_down().start())
    for s in range(s_local):
        if s == s_local - 1:
            for d in range(1, peers):
                when(active(up(d)), lambda: window(d).start())
        targets(lambda d: gather(s, d).start(), near if s else far)
        gather(s, None).start()

    def complete(s):
        remote(
            gat.at[s, partner], gat.at[s, partner], ag_send_sem.at[s, 0], ag_recv_sem.at[s, 0], (e, partner, r)
        ).wait_recv()
        for d in range(1, chips):
            src = lax.rem(partner + n_c - 2 * d, n_c)
            remote(
                gat.at[s, src], gat.at[s, src], f_send_sem.at[s, d], f_recv_sem.at[s, d], (e, partner, r)
            ).wait_recv()

    count = filters.shape[-1]
    slices = s_local * n_r
    band = pen_send.shape[3]
    for load in loads[1:4]:
        load.wait()
    flat_filters = filters[...].astype(F32).reshape(-1, count).astype(BF16)
    pieces = [dot(spread[at], flat_filters) for at in range(slices)]
    for at in range(slices):
        wide_ref[:, at * count : (at + 1) * count] = pieces[at].astype(BF16)
        tall_ref[at * count : (at + 1) * count, :] = pieces[at].T.astype(BF16)
    shape = (slices, count, count)
    on = lax.broadcasted_iota(jnp.int32, shape, 1) == lax.broadcasted_iota(jnp.int32, shape, 2)
    column = jnp.sum(jnp.where(on, thr[...].reshape(1, 1, count), 0.0), axis=2, keepdims=True)
    level[...] = jnp.broadcast_to(column, (slices, count, zp)).reshape(slices * count, zp)

    def prepare():
        ext[e, r] = padded[pl.ds((1 + q) * rq, rq + 4)]
        for d in range(1, peers):
            src = down(d)
            remote(
                padded.at[pl.ds(0, rq + 4)], ext.at[src // n_r, lax.rem(src, n_r)], x_send_sem.at[d], x_recv_sem.at[d], (e, c, r)
            ).wait_recv()

        def border(which, begin):
            for src in range(peers):
                at = (which, src // n_r, src % n_r)
                remote(
                    padded.at[pl.ds(0, 2)], edge.at[at], e_send_sem.at[0], e_recv_sem.at[which, src], (e, c, r)
                ).wait_recv()
                ext[src // n_r, src % n_r, begin : begin + 2] = edge[at]

        pl.when(jnp.logical_and(q == 0, c > 0))(lambda: border(0, 0))
        pl.when(jnp.logical_and(q == last, c < n_c - 1))(lambda: border(1, rq + 2))

        rows = rq + 4
        taps = 2 * s_local * n_r
        for echo in range(n_e):
            parts = [ext[echo, read].astype(F32) for read in range(n_r)]
            block = jnp.concatenate(parts, axis=1) if n_r > 1 else parts[0]
            flat = block.reshape(rows * taps, zp)
            moved = [
                pltpu.roll(flat, 1, 1).reshape(rows, taps, zp),
                block,
                pltpu.roll(flat, zp - 1, 1).reshape(rows, taps, zp),
            ]
            fill = [jnp.zeros((rows, SLAB - 3 * taps, zp), F32)] if SLAB > 3 * taps else []
            slab[echo] = jnp.concatenate(moved + fill, axis=1).reshape(rows * SLAB, zp).astype(BF16)

        pacc[...] = jnp.zeros_like(pacc)

    def respond(begin, end):
        tall = tall_ref[...]
        wide = wide_ref[...]
        first = c * rb + q * rq - 1

        for i in range(begin, end):
            window = slice(i * SLAB, (i + 3) * SLAB)
            response = [dot(tall, slab[echo, window, :]) for echo in range(n_e)]
            energy = response[0] * response[0]
            for other in response[1:]:
                energy = energy + other * other
            factor = 1.0 / (1.0 + level[...] * lax.rsqrt(jnp.maximum(energy, TINY)))
            if i in (0, rq + 1):
                inside = jnp.logical_and(first + i >= 0, first + i < ny)
                factor = jnp.where(inside, factor, 0.0)
            for echo in range(n_e):
                spread = dot(wide, (response[echo] * factor).astype(BF16))
                for a in range(3):
                    pacc[echo, i + a] += spread[a * SLAB : (a + 1) * SLAB]

    def collect():
        taps = 2 * s_local * n_r
        lane = lax.broadcasted_iota(jnp.int32, (1, 1, zp), 2)
        for echo in range(n_e):
            held = pacc[echo, 2 : 2 + rq]
            low = pltpu.roll(held[:, :taps].reshape(rq * taps, zp), zp - 1, 1).reshape(rq, taps, zp)
            high = pltpu.roll(held[:, 2 * taps : 3 * taps].reshape(rq * taps, zp), 1, 1).reshape(rq, taps, zp)
            low = jnp.where(lane < nz - 1, low, 0.0)
            high = jnp.where(lane > 0, high, 0.0)
            total = low + held[:, taps : 2 * taps] + high
            for read in range(n_r):
                own = range(read * 2 * s_local, (read + 1) * 2 * s_local)
                dense = jnp.concatenate([total[:, k, :nz] for k in own], axis=1)
                for k in range(rq // band):
                    pen_send[echo, read, k] = dense[k * band : (k + 1) * band]
        pen_recv[q] = pen_send[e, r]

    def penalty_out(d):
        to = up(d)
        return remote(
            pen_send.at[to // n_r, lax.rem(to, n_r)], pen_recv.at[q], p_send_sem.at[d], p_recv_sem.at[d],
            (to // n_r, c, lax.rem(to, n_r)),
        )

    marks = [0] + [(rq + 2) * part // 14 for part in SPLITS] + [rq + 2]

    def rows(at):
        def act():
            if at == 0:
                prepare()
            respond(marks[at], marks[at + 1])
            if at == len(marks) - 2:
                collect()
                for d in range(1, peers):
                    penalty_out(d).start()

        when(active(q), act)

    def turn():
        for load in loads[4:]:
            load.wait()
        for buf in (k_rows, m_rows, weighted):
            buf[...] = jnp.zeros_like(buf)
        for s in range(s_local):
            for p in range(2):
                at = slice(p * zp, p * zp + nz)
                k_rows[s, :, at] = kspace[s, p].astype(F32).T.astype(BF16)
                m_rows[s, :, at] = maps[s, p].astype(F32).T.astype(BF16)
        s_rows[:, :nz] = samp[...].astype(F32).T
        s_rows[:, nz:] = jnp.zeros((ny, zp - nz), F32)

    def halves(j):
        return side if j == 0 else 1 - side

    def pair(s, j):
        h = halves(j)
        return remote(
            part.at[s, h, :, 1 - core], paired.at[s, h], pair_send_sem.at[s, j], pair_recv_sem.at[s, j],
            (e, partner, r),
        )

    def scatter(s, to):
        d = lax.rem(to - chip + chips, chips)
        return remote(
            rs_send.at[s, to], rs_recv.at[s, chip], rs_send_sem.at[s, d], rs_recv_sem.at[s, d],
            (e, 2 * to + core, r),
        )

    def send_sums(s, j):
        pair(s, j).wait_recv()
        h = halves(j)
        sums = (part[s, h, :, core].astype(F32) + paired[s, h].astype(F32)).astype(BF16)
        for k in range(group):
            rs_send[s, h * group + k] = sums[k]
        for k in range(group):
            to = h * group + jnp.where(h == 1, group - 1 - k, k)
            if j:
                pl.when(to != chip)(lambda: scatter(s, to).start())
            else:
                scatter(s, to).start()

    def swapped(x, sign):
        low, high = x[:, :zp], x[:, zp:]
        return jnp.concatenate([high, -low] if sign > 0 else [-high, low], axis=1)

    def columns(s, which):
        starts = [pl.multiple_of((2 * k + which) * rb, 8) for k in range(chips)]
        image = jnp.concatenate([gat[s, 2 * k + which] for k in range(chips)], axis=0)
        sense = jnp.concatenate([m_rows[s, pl.ds(at, rb), :] for at in starts], axis=0)
        real, imag = image[:, :nz].astype(F32), image[:, nz:].astype(F32)
        map_real, map_imag = sense[:, :nz].astype(F32), sense[:, zp : zp + nz].astype(F32)
        weighted[:half, :nz] = (map_real * real - map_imag * imag).astype(BF16)
        weighted[:half, zp : zp + nz] = (map_real * imag + map_imag * real).astype(BF16)
        halfway = dot(weighted[:half, :], fz[...])
        upper, lower = halfway.astype(BF16), swapped(halfway, 1).astype(BF16)
        for k, at in enumerate(starts):
            stack[pl.ds(at, rb), :] = upper[k * rb : (k + 1) * rb]
            stack[pl.ds(ny + at, rb), :] = lower[k * rb : (k + 1) * rb]

    def fronts(s):
        spectrum = dot(ty[...], stack[...])
        sampled = s_rows[...]
        sampled = jnp.concatenate([sampled, sampled], axis=1)
        residual = sampled * (spectrum - k_rows[s].astype(F32))
        stack[:ny] = residual.astype(BF16)
        stack[ny:] = swapped(residual, -1).astype(BF16)

    def middle():
        weighted[...] = dot(ty[...], stack[...]).astype(BF16)

    def backs(s, j):
        h = halves(j)
        at = pl.ds(pl.multiple_of(h * half, 16), half)
        restored = dot(weighted[at, :], az[...])
        back_real, back_imag = restored[:, :nz], restored[:, zp : zp + nz]
        map_real, map_imag = m_rows[s, at, :nz].astype(F32), m_rows[s, at, zp : zp + nz].astype(F32)
        adjoint = jnp.concatenate(
            [
                (map_real * back_real + map_imag * back_imag).astype(BF16),
                (map_real * back_imag - map_imag * back_real).astype(BF16),
            ],
            axis=1,
        )
        part[s, h] = adjoint.reshape(group, 2, rb, width)
        pair(s, j).start()

    turn()
    rows(0)
    relay(0, near)
    columns(0, core)
    complete(0)
    columns(0, 1 - core)
    fronts(0)
    middle()
    backs(0, 0)
    relay(1, near)
    backs(0, 1)
    columns(1, core)
    rows(1)
    send_sums(0, 0)
    complete(1)
    columns(1, 1 - core)
    send_sums(0, 1)
    fronts(1)
    middle()
    backs(1, 0)
    backs(1, 1)
    rows(2)
    send_sums(1, 0)
    rows(3)
    send_sums(1, 1)
    rows(4)

    def wait_pen():
        for d in range(1, peers):
            src = down(d)
            when(
                active(src),
                lambda: remote(
                    pen_send.at[0, 0], pen_recv.at[src], p_send_sem.at[d], p_recv_sem.at[d], (e, c, r)
                ).wait_recv(),
            )
        for at in range(n_q):
            for k in range(rq // band):
                row = at * rq + k * band
                flat[row : row + band, :] = flat[row : row + band, :] - pen_recv[at, k]

    def hops(s):
        for d in range(1, chips):
            src = lax.rem(chip + chips - d, chips)
            remote(
                rs_send.at[s, src], rs_recv.at[s, src], rs_send_sem.at[s, d], rs_recv_sem.at[s, d], (e, partner, r)
            ).wait_recv()

    def finish(s):
        mine, slot = chip // group, lax.rem(chip, group)
        total = part[s, mine, slot, core].astype(F32) + paired[s, mine, slot].astype(F32)
        for d in range(1, chips):
            total = total + rs_recv[s, lax.rem(chip + chips - d, chips)].astype(F32)
        at = slice(s * width, (s + 1) * width)
        out_ref[:, at] = flat[:, at] - dc_ref[0] * total

    wait_pen()
    for s in range(s_local):
        hops(s)
        finish(s)

    for s in range(s_local):
        gather(s, None).wait_send()
        for d in range(1, chips):
            gather(s, d).wait_send()
            forward(s, d).wait_send()
            scatter(s, lax.rem(chip + d, chips)).wait_send()
    for s in range(s_local):
        for j in range(2):
            pair(s, j).wait_send()
    for d in range(1, peers):
        when(active(up(d)), lambda: window(d).wait_send())
        when(active(q), lambda: penalty_out(d).wait_send())
    pl.when(c < n_c - 1)(lambda: edge_up().wait_send())
    pl.when(c > 0)(lambda: edge_down().wait_send())


def body(kspace, sampling, coil_maps, image, filters, thresholds, dc_weight):
    n_e, n_c, n_r = lax.axis_size("echo"), lax.axis_size("coil"), lax.axis_size("read")
    rb, _, s_local, _, nz = image.shape
    ny = kspace.shape[0]
    peers = n_e * n_r
    rq = window_rows(rb, peers)
    n_q = rb // rq
    zp = -(-(nz + 1) // 128) * 128
    width = 2 * nz
    slices = s_local * n_r
    taps = 2 * slices
    band = math.gcd(rq, 4)
    count = filters.shape[0]

    col_cos, col_sin = tables(nz)
    row_cos, row_sin = tables(ny)
    gap = ((0, zp - nz), (0, zp - nz))
    col_cos, col_sin = np.pad(col_cos, gap), np.pad(col_sin, gap)
    fz = jnp.asarray(np.block([[col_cos, -col_sin], [col_sin, col_cos]]), BF16)
    az = jnp.asarray(np.block([[col_cos, col_sin], [-col_sin, col_cos]]), BF16)
    ty = jnp.asarray(np.concatenate([row_cos, row_sin], 1), BF16)

    spread = np.zeros((slices, 3, SLAB, 3, 3, 3, 2))
    for at in range(slices):
        for a in range(3):
            for b in range(3):
                for d in range(3):
                    for p in range(2):
                        if 0 <= at + b - 1 < slices:
                            spread[at, a, d * taps + (at + b - 1) * 2 + p, a, b, d, p] = 1.0
    spread = jnp.asarray(spread.reshape(slices, 3 * SLAB, 54), BF16)

    k_view = jnp.transpose(kspace[:, 0, 0], (1, 2, 3, 0))
    m_view = jnp.transpose(coil_maps[:, 0], (1, 2, 3, 0))
    s_view = jnp.transpose(sampling[:, 0], (1, 0))

    operands = tuple(
        pltpu.with_memory_space_constraint(x, pltpu.HBM)
        for x in (
            image[:, 0], spread, jnp.transpose(filters, (1, 2, 3, 4, 0)), thresholds[None, :],
            k_view, m_view, s_view, fz, az, ty,
        )
    )
    vmem = pl.BlockSpec(memory_space=pltpu.VMEM)
    hbm = pl.BlockSpec(memory_space=pltpu.HBM)
    smem = pl.BlockSpec(memory_space=pltpu.SMEM)
    dma = pltpu.SemaphoreType.DMA
    updated = pl.pallas_call(
        functools.partial(kernel, (n_e, n_c, n_r, n_q, rq, nz, ny)),
        out_shape=jax.ShapeDtypeStruct((rb, s_local * width), F32),
        in_specs=[hbm] * 4 + [smem] + [hbm] * 6,
        out_specs=vmem,
        scratch_shapes=[
            pltpu.VMEM((rb, s_local, 2, nz), F32),
            pltpu.VMEM((rb, s_local * width), F32),
            pltpu.VMEM((rb + 2 * (rq + 2), 2 * s_local, zp), BF16),
            pltpu.VMEM(spread.shape, BF16),
            pltpu.VMEM((3, 3, 3, 2, count), BF16),
            pltpu.VMEM((1, count), F32),
            pltpu.VMEM((s_local, n_c, rb, width), BF16),
            pltpu.VMEM((s_local, 2, n_c // 4, 2, rb, width), BF16),
            pltpu.VMEM((s_local, 2, n_c // 4, rb, width), BF16),
            pltpu.VMEM((s_local, n_c // 2, rb, width), BF16),
            pltpu.VMEM((s_local, n_c // 2, rb, width), BF16),
            pltpu.VMEM((3 * SLAB, slices * count), BF16),
            pltpu.VMEM((slices * count, 3 * SLAB), BF16),
            pltpu.VMEM((slices * count, zp), F32),
            pltpu.VMEM((n_e, n_r, rq + 4, 2 * s_local, zp), BF16),
            pltpu.VMEM((2, n_e, n_r, 2, 2 * s_local, zp), BF16),
            pltpu.VMEM((n_e, n_r, rq // band, band, s_local * width), F32),
            pltpu.VMEM((n_q, rq // band, band, s_local * width), F32),
            pltpu.VMEM((n_e, rq + 4, SLAB, zp), F32),
            pltpu.VMEM((n_e, (rq + 4) * SLAB, zp), BF16),
            pltpu.VMEM(k_view.shape, BF16),
            pltpu.VMEM(m_view.shape, BF16),
            pltpu.VMEM(s_view.shape, jnp.int32),
            pltpu.VMEM(fz.shape, BF16),
            pltpu.VMEM(az.shape, BF16),
            pltpu.VMEM(ty.shape, BF16),
            pltpu.VMEM((s_local, ny, 2 * zp), BF16),
            pltpu.VMEM((s_local, ny, 2 * zp), BF16),
            pltpu.VMEM((ny, zp), F32),
            pltpu.VMEM((ny, 2 * zp), BF16),
            pltpu.VMEM((2 * ny, 2 * zp), BF16),
            dma((10,)),
            dma((s_local, n_c)), dma((s_local, n_c)),
            dma((peers,)), dma((peers,)),
            dma((2,)), dma((2, peers)),
            dma((peers,)), dma((peers,)),
            dma((s_local, n_c)), dma((s_local, n_c)),
            dma((s_local, n_c)), dma((s_local, n_c)), dma((s_local, 2)), dma((s_local, 2)),
        ],
        compiler_params=pltpu.CompilerParams(
            collective_id=0, has_side_effects=True, vmem_limit_bytes=GRANT
        ),
        name="cascade",
    )(*operands[:4], dc_weight, *operands[4:])
    return updated.reshape(image.shape)


def solution(mesh):
    return jax.shard_map(
        body,
        mesh=mesh,
        in_specs=(
            P(None, "echo", "coil", "read", None, None),
            P(None, "echo", None),
            P(None, "coil", "read", None, None),
            P("coil", "echo", "read", None, None),
            P(),
            P(),
            P("echo"),
        ),
        out_specs=P("coil", "echo", "read", None, None),
        check_vma=False,
    )
```

```python
import functools
import math

import numpy as np
import jax
import jax.numpy as jnp
from jax import lax
from jax.experimental import pallas as pl
from jax.experimental.pallas import tpu as pltpu
from jax.sharding import PartitionSpec as P

MESH = pl.DeviceIdType.MESH
F32 = jnp.float32
BF16 = jnp.bfloat16
SLAB = 32
GRANT = 24 << 20
TINY = float(np.finfo(np.float32).tiny)
SPLITS = (7, 7, 11, 11)


def tables(length):
    product = np.outer(np.arange(length), np.arange(length)) % length
    phases = product * (2.0 * np.pi / length)
    normalize = length ** (-0.5)
    return np.cos(phases) * normalize, np.sin(phases) * normalize


def window_rows(rows, peers):
    for size in range(2, rows + 1):
        if rows % size == 0 and rows // size <= peers:
            return size
    return rows


def dot(left, right):
    return jnp.dot(left, right, preferred_element_type=F32)


def kernel(
    cfg,
    image_hbm, spread_hbm, filters_hbm, thr_hbm, dc_ref, kspace_hbm, maps_hbm, samp_hbm, fz_hbm, az_hbm, ty_hbm,
    out_ref,
    image, flat, padded, spread, filters, thr,
    gat, part, paired, rs_send, rs_recv, wide_ref, tall_ref, level, ext, edge, pen_send, pen_recv, pacc, slab,
    kspace, maps, samp, fz, az, ty, k_rows, m_rows, s_rows, weighted, stack,
    local_sem, ag_send_sem, ag_recv_sem, x_send_sem, x_recv_sem, e_send_sem, e_recv_sem,
    p_send_sem, p_recv_sem, rs_send_sem, rs_recv_sem, f_send_sem, f_recv_sem, pair_send_sem, pair_recv_sem,
):
    n_e, n_c, n_r, n_q, rq, nz, ny = cfg
    peers = n_e * n_r
    e = lax.axis_index("echo")
    c = lax.axis_index("coil")
    r = lax.axis_index("read")
    q = e * n_r + r
    s_local, rb = rs_send.shape[0], flat.shape[0]
    chips = n_c // 2
    core = lax.rem(c, 2)
    chip = c // 2
    partner = c + 1 - 2 * core
    width = 2 * nz
    zp = ext.shape[-1]
    half = ny // 2
    group = chips // 2
    side = jnp.where(chip < group, 1, 0)

    loads = [
        pltpu.make_async_copy(src, dst, local_sem.at[i])
        for i, (src, dst) in enumerate(
            [
                (image_hbm, image), (spread_hbm, spread), (filters_hbm, filters), (thr_hbm, thr),
                (maps_hbm, maps), (fz_hbm, fz), (ty_hbm, ty), (kspace_hbm, kspace), (samp_hbm, samp), (az_hbm, az),
            ]
        )
    ]

    for load in loads:
        load.start()

    def remote(src, dst, send, recv, target):
        return pltpu.make_async_remote_copy(
            src_ref=src, dst_ref=dst, send_sem=send, recv_sem=recv, device_id=target, device_id_type=MESH
        )

    def when(condition, act):
        if condition is True:
            act()
        else:
            pl.when(condition)(act)

    def up(d):
        return lax.rem(q + d, peers)

    def down(d):
        return lax.rem(q + peers - d, peers)

    def active(which):
        return True if n_q == peers else which < n_q

    barrier = pltpu.get_barrier_semaphore()
    for d in range(chips):
        to = lax.rem(c + 2 * d, n_c) if d else partner
        pl.semaphore_signal(barrier, inc=1, device_id=(e, to, r), device_id_type=MESH)
    for d in range(1, peers):
        pl.semaphore_signal(barrier, inc=1, device_id=(up(d) // n_r, c, lax.rem(up(d), n_r)), device_id_type=MESH)
    last = n_q - 1

    def greet(step):
        for at in range(peers):
            pl.semaphore_signal(barrier, inc=1, device_id=(at // n_r, c + step, at % n_r), device_id_type=MESH)

    pl.when(jnp.logical_and(q == 0, c > 0))(lambda: greet(-1))
    pl.when(jnp.logical_and(q == last, c < n_c - 1))(lambda: greet(1))
    margin = rq + 2
    padded[...] = jnp.zeros_like(padded)
    loads[0].wait()
    flat[...] = jnp.concatenate([image[:, s, p, :] for s in range(s_local) for p in range(2)], axis=1)
    for s in range(s_local):
        gat[s, c] = flat[:, s * width : (s + 1) * width].astype(BF16)

    padded[margin : margin + rb, :, :nz] = image[...].reshape(rb, 2 * s_local, nz).astype(BF16)
    sides = jnp.minimum(c, 1) + jnp.minimum(n_c - 1 - c, 1)
    pl.semaphore_wait(barrier, chips + peers - 1 + sides)

    def window(d):
        to = up(d)
        return remote(
            padded.at[pl.ds((1 + to) * rq, rq + 4)], ext.at[e, r], x_send_sem.at[d], x_recv_sem.at[d], (to // n_r, c, lax.rem(to, n_r))
        )

    def edge_up():
        return remote(
            padded.at[pl.ds(margin + rb - 2, 2)], edge.at[0, e, r], e_send_sem.at[0], e_recv_sem.at[0, q], (0, c + 1, 0)
        )

    def edge_down():
        return remote(
            padded.at[pl.ds(margin, 2)], edge.at[1, e, r], e_send_sem.at[1], e_recv_sem.at[1, q],
            (last // n_r, c - 1, last % n_r),
        )

    def gather(s, d):
        to = lax.rem(c + 2 * d, n_c) if d is not None else partner
        at = 0 if d is None else d
        return remote(gat.at[s, c], gat.at[s, c], ag_send_sem.at[s, at], ag_recv_sem.at[s, at], (e, to, r))

    def gathered(s, d):
        src = lax.rem(c + n_c - 2 * d, n_c)
        return remote(gat.at[s, src], gat.at[s, src], ag_send_sem.at[s, d], ag_recv_sem.at[s, d], (e, partner, r))

    def forward(s, d):
        src = lax.rem(c + n_c - 2 * d, n_c)
        return remote(gat.at[s, src], gat.at[s, src], f_send_sem.at[s, d], f_recv_sem.at[s, d], (e, partner, r))

    def targets(act, dists):
        for dist in dists:
            pl.when(chip + dist < chips)(lambda: act(dist))
            pl.when(chip - dist >= 0)(lambda: act(chips - dist))

    def relay(s, dists):
        def one(d):
            gathered(s, d).wait_recv()
            forward(s, d).start()

        for dist in dists:
            pl.when(chip - dist >= 0)(lambda: one(dist))
            pl.when(chip + dist < chips)(lambda: one(chips - dist))

    near = range(1, chips)
    far = near[::-1]

    pl.when(c < n_c - 1)(lambda: edge_up().start())
    pl.when(c > 0)(lambda: edge_down().start())
    for s in range(s_local):
        if s == s_local - 1:
            for d in range(1, peers):
                when(active(up(d)), lambda: window(d).start())
        targets(lambda d: gather(s, d).start(), near if s else far)
        gather(s, None).start()

    def complete(s):
        remote(
            gat.at[s, partner], gat.at[s, partner], ag_send_sem.at[s, 0], ag_recv_sem.at[s, 0], (e, partner, r)
        ).wait_recv()
        for d in range(1, chips):
            src = lax.rem(partner + n_c - 2 * d, n_c)
            remote(
                gat.at[s, src], gat.at[s, src], f_send_sem.at[s, d], f_recv_sem.at[s, d], (e, partner, r)
            ).wait_recv()

    count = filters.shape[-1]
    slices = s_local * n_r
    band = pen_send.shape[3]
    for load in loads[1:4]:
        load.wait()
    flat_filters = filters[...].astype(F32).reshape(-1, count).astype(BF16)
    pieces = [dot(spread[at], flat_filters) for at in range(slices)]
    for at in range(slices):
        wide_ref[:, at * count : (at + 1) * count] = pieces[at].astype(BF16)
        tall_ref[at * count : (at + 1) * count, :] = pieces[at].T.astype(BF16)
    shape = (slices, count, count)
    on = lax.broadcasted_iota(jnp.int32, shape, 1) == lax.broadcasted_iota(jnp.int32, shape, 2)
    column = jnp.sum(jnp.where(on, thr[...].reshape(1, 1, count), 0.0), axis=2, keepdims=True)
    level[...] = jnp.broadcast_to(column, (slices, count, zp)).reshape(slices * count, zp)

    def prepare():
        ext[e, r] = padded[pl.ds((1 + q) * rq, rq + 4)]
        for d in range(1, peers):
            src = down(d)
            remote(
                padded.at[pl.ds(0, rq + 4)], ext.at[src // n_r, lax.rem(src, n_r)], x_send_sem.at[d], x_recv_sem.at[d], (e, c, r)
            ).wait_recv()

        def border(which, begin):
            for src in range(peers):
                at = (which, src // n_r, src % n_r)
                remote(
                    padded.at[pl.ds(0, 2)], edge.at[at], e_send_sem.at[0], e_recv_sem.at[which, src], (e, c, r)
                ).wait_recv()
                ext[src // n_r, src % n_r, begin : begin + 2] = edge[at]

        pl.when(jnp.logical_and(q == 0, c > 0))(lambda: border(0, 0))
        pl.when(jnp.logical_and(q == last, c < n_c - 1))(lambda: border(1, rq + 2))

        rows = rq + 4
        taps = 2 * s_local * n_r
        for echo in range(n_e):
            parts = [ext[echo, read].astype(F32) for read in range(n_r)]
            block = jnp.concatenate(parts, axis=1) if n_r > 1 else parts[0]
            flat = block.reshape(rows * taps, zp)
            moved = [
                pltpu.roll(flat, 1, 1).reshape(rows, taps, zp),
                block,
                pltpu.roll(flat, zp - 1, 1).reshape(rows, taps, zp),
            ]
            fill = [jnp.zeros((rows, SLAB - 3 * taps, zp), F32)] if SLAB > 3 * taps else []
            slab[echo] = jnp.concatenate(moved + fill, axis=1).reshape(rows * SLAB, zp).astype(BF16)

        pacc[...] = jnp.zeros_like(pacc)

    def respond(begin, end):
        tall = tall_ref[...]
        wide = wide_ref[...]
        first = c * rb + q * rq - 1

        for i in range(begin, end):
            window = slice(i * SLAB, (i + 3) * SLAB)
            response = [dot(tall, slab[echo, window, :]) for echo in range(n_e)]
            energy = response[0] * response[0]
            for other in response[1:]:
                energy = energy + other * other
            factor = 1.0 / (1.0 + level[...] * lax.rsqrt(jnp.maximum(energy, TINY)))
            if i in (0, rq + 1):
                inside = jnp.logical_and(first + i >= 0, first + i < ny)
                factor = jnp.where(inside, factor, 0.0)
            for echo in range(n_e):
                spread = dot(wide, (response[echo] * factor).astype(BF16))
                for a in range(3):
                    pacc[echo, i + a] += spread[a * SLAB : (a + 1) * SLAB]

    def collect():
        taps = 2 * s_local * n_r
        lane = lax.broadcasted_iota(jnp.int32, (1, 1, zp), 2)
        for echo in range(n_e):
            held = pacc[echo, 2 : 2 + rq]
            low = pltpu.roll(held[:, :taps].reshape(rq * taps, zp), zp - 1, 1).reshape(rq, taps, zp)
            high = pltpu.roll(held[:, 2 * taps : 3 * taps].reshape(rq * taps, zp), 1, 1).reshape(rq, taps, zp)
            low = jnp.where(lane < nz - 1, low, 0.0)
            high = jnp.where(lane > 0, high, 0.0)
            total = low + held[:, taps : 2 * taps] + high
            for read in range(n_r):
                own = range(read * 2 * s_local, (read + 1) * 2 * s_local)
                dense = jnp.concatenate([total[:, k, :nz] for k in own], axis=1)
                for k in range(rq // band):
                    pen_send[echo, read, k] = dense[k * band : (k + 1) * band]
        pen_recv[q] = pen_send[e, r]

    def penalty_out(d):
        to = up(d)
        return remote(
            pen_send.at[to // n_r, lax.rem(to, n_r)], pen_recv.at[q], p_send_sem.at[d], p_recv_sem.at[d],
            (to // n_r, c, lax.rem(to, n_r)),
        )

    marks = [0] + [(rq + 2) * part // 14 for part in SPLITS] + [rq + 2]

    def rows(at):
        def act():
            if at == 0:
                prepare()
            respond(marks[at], marks[at + 1])
            if at == len(marks) - 2:
                collect()
                for d in range(1, peers):
                    penalty_out(d).start()

        when(active(q), act)

    def turn():
        for load in loads[4:]:
            load.wait()
        for buf in (k_rows, m_rows, weighted):
            buf[...] = jnp.zeros_like(buf)
        for s in range(s_local):
            for p in range(2):
                at = slice(p * zp, p * zp + nz)
                k_rows[s, :, at] = kspace[s, p].astype(F32).T.astype(BF16)
                m_rows[s, :, at] = maps[s, p].astype(F32).T.astype(BF16)
        s_rows[:, :nz] = samp[...].astype(F32).T
        s_rows[:, nz:] = jnp.zeros((ny, zp - nz), F32)

    def halves(j):
        return side if j == 0 else 1 - side

    def pair(s, j):
        h = halves(j)
        return remote(
            part.at[s, h, :, 1 - core], paired.at[s, h], pair_send_sem.at[s, j], pair_recv_sem.at[s, j],
            (e, partner, r),
        )

    def scatter(s, to):
        d = lax.rem(to - chip + chips, chips)
        return remote(
            rs_send.at[s, to], rs_recv.at[s, chip], rs_send_sem.at[s, d], rs_recv_sem.at[s, d],
            (e, 2 * to + core, r),
        )

    def send_sums(s, j):
        pair(s, j).wait_recv()
        h = halves(j)
        sums = (part[s, h, :, core].astype(F32) + paired[s, h].astype(F32)).astype(BF16)
        for k in range(group):
            rs_send[s, h * group + k] = sums[k]
        for k in range(group):
            to = h * group + jnp.where(h == 1, group - 1 - k, k)
            if j:
                pl.when(to != chip)(lambda: scatter(s, to).start())
            else:
                scatter(s, to).start()

    def swapped(x, sign):
        low, high = x[:, :zp], x[:, zp:]
        return jnp.concatenate([high, -low] if sign > 0 else [-high, low], axis=1)

    def columns(s, which):
        starts = [pl.multiple_of((2 * k + which) * rb, 8) for k in range(chips)]
        image = jnp.concatenate([gat[s, 2 * k + which] for k in range(chips)], axis=0)
        sense = jnp.concatenate([m_rows[s, pl.ds(at, rb), :] for at in starts], axis=0)
        real, imag = image[:, :nz].astype(F32), image[:, nz:].astype(F32)
        map_real, map_imag = sense[:, :nz].astype(F32), sense[:, zp : zp + nz].astype(F32)
        weighted[:half, :nz] = (map_real * real - map_imag * imag).astype(BF16)
        weighted[:half, zp : zp + nz] = (map_real * imag + map_imag * real).astype(BF16)
        halfway = dot(weighted[:half, :], fz[...])
        upper, lower = halfway.astype(BF16), swapped(halfway, 1).astype(BF16)
        for k, at in enumerate(starts):
            stack[pl.ds(at, rb), :] = upper[k * rb : (k + 1) * rb]
            stack[pl.ds(ny + at, rb), :] = lower[k * rb : (k + 1) * rb]

    def fronts(s):
        spectrum = dot(ty[...], stack[...])
        sampled = s_rows[...]
        sampled = jnp.concatenate([sampled, sampled], axis=1)
        residual = sampled * (spectrum - k_rows[s].astype(F32))
        stack[:ny] = residual.astype(BF16)
        stack[ny:] = swapped(residual, -1).astype(BF16)

    def middle():
        weighted[...] = dot(ty[...], stack[...]).astype(BF16)

    def backs(s, j):
        h = halves(j)
        at = pl.ds(pl.multiple_of(h * half, 16), half)
        restored = dot(weighted[at, :], az[...])
        back_real, back_imag = restored[:, :nz], restored[:, zp : zp + nz]
        map_real, map_imag = m_rows[s, at, :nz].astype(F32), m_rows[s, at, zp : zp + nz].astype(F32)
        adjoint = jnp.concatenate(
            [
                (map_real * back_real + map_imag * back_imag).astype(BF16),
                (map_real * back_imag - map_imag * back_real).astype(BF16),
            ],
            axis=1,
        )
        part[s, h] = adjoint.reshape(group, 2, rb, width)
        pair(s, j).start()

    turn()
    rows(0)
    relay(0, near)
    columns(0, core)
    complete(0)
    columns(0, 1 - core)
    fronts(0)
    middle()
    backs(0, 0)
    relay(1, near)
    backs(0, 1)
    columns(1, core)
    rows(1)
    send_sums(0, 0)
    complete(1)
    columns(1, 1 - core)
    send_sums(0, 1)
    fronts(1)
    middle()
    backs(1, 0)
    backs(1, 1)
    rows(2)
    send_sums(1, 0)
    rows(3)
    send_sums(1, 1)
    rows(4)

    def wait_pen():
        for d in range(1, peers):
            src = down(d)
            when(
                active(src),
                lambda: remote(
                    pen_send.at[0, 0], pen_recv.at[src], p_send_sem.at[d], p_recv_sem.at[d], (e, c, r)
                ).wait_recv(),
            )
        for at in range(n_q):
            for k in range(rq // band):
                row = at * rq + k * band
                flat[row : row + band, :] = flat[row : row + band, :] - pen_recv[at, k]

    def hops(s):
        for d in range(1, chips):
            src = lax.rem(chip + chips - d, chips)
            remote(
                rs_send.at[s, src], rs_recv.at[s, src], rs_send_sem.at[s, d], rs_recv_sem.at[s, d], (e, partner, r)
            ).wait_recv()

    def finish(s):
        mine, slot = chip // group, lax.rem(chip, group)
        total = part[s, mine, slot, core].astype(F32) + paired[s, mine, slot].astype(F32)
        for d in range(1, chips):
            total = total + rs_recv[s, lax.rem(chip + chips - d, chips)].astype(F32)
        at = slice(s * width, (s + 1) * width)
        out_ref[:, at] = flat[:, at] - dc_ref[0] * total

    wait_pen()
    for s in range(s_local):
        hops(s)
        finish(s)

    for s in range(s_local):
        gather(s, None).wait_send()
        for d in range(1, chips):
            gather(s, d).wait_send()
            forward(s, d).wait_send()
            scatter(s, lax.rem(chip + d, chips)).wait_send()
    for s in range(s_local):
        for j in range(2):
            pair(s, j).wait_send()
    for d in range(1, peers):
        when(active(up(d)), lambda: window(d).wait_send())
        when(active(q), lambda: penalty_out(d).wait_send())
    pl.when(c < n_c - 1)(lambda: edge_up().wait_send())
    pl.when(c > 0)(lambda: edge_down().wait_send())


def body(kspace, sampling, coil_maps, image, filters, thresholds, dc_weight):
    n_e, n_c, n_r = lax.axis_size("echo"), lax.axis_size("coil"), lax.axis_size("read")
    rb, _, s_local, _, nz = image.shape
    ny = kspace.shape[0]
    peers = n_e * n_r
    rq = window_rows(rb, peers)
    n_q = rb // rq
    zp = -(-(nz + 1) // 128) * 128
    width = 2 * nz
    slices = s_local * n_r
    taps = 2 * slices
    band = math.gcd(rq, 4)
    count = filters.shape[0]

    col_cos, col_sin = tables(nz)
    row_cos, row_sin = tables(ny)
    gap = ((0, zp - nz), (0, zp - nz))
    col_cos, col_sin = np.pad(col_cos, gap), np.pad(col_sin, gap)
    fz = jnp.asarray(np.block([[col_cos, -col_sin], [col_sin, col_cos]]), BF16)
    az = jnp.asarray(np.block([[col_cos, col_sin], [-col_sin, col_cos]]), BF16)
    ty = jnp.asarray(np.concatenate([row_cos, row_sin], 1), BF16)

    spread = np.zeros((slices, 3, SLAB, 3, 3, 3, 2))
    for at in range(slices):
        for a in range(3):
            for b in range(3):
                for d in range(3):
                    for p in range(2):
                        if 0 <= at + b - 1 < slices:
                            spread[at, a, d * taps + (at + b - 1) * 2 + p, a, b, d, p] = 1.0
    spread = jnp.asarray(spread.reshape(slices, 3 * SLAB, 54), BF16)

    k_view = jnp.transpose(kspace[:, 0, 0], (1, 2, 3, 0))
    m_view = jnp.transpose(coil_maps[:, 0], (1, 2, 3, 0))
    s_view = jnp.transpose(sampling[:, 0], (1, 0))

    operands = tuple(
        pltpu.with_memory_space_constraint(x, pltpu.HBM)
        for x in (
            image[:, 0], spread, jnp.transpose(filters, (1, 2, 3, 4, 0)), thresholds[None, :],
            k_view, m_view, s_view, fz, az, ty,
        )
    )
    vmem = pl.BlockSpec(memory_space=pltpu.VMEM)
    hbm = pl.BlockSpec(memory_space=pltpu.HBM)
    smem = pl.BlockSpec(memory_space=pltpu.SMEM)
    dma = pltpu.SemaphoreType.DMA
    updated = pl.pallas_call(
        functools.partial(kernel, (n_e, n_c, n_r, n_q, rq, nz, ny)),
        out_shape=jax.ShapeDtypeStruct((rb, s_local * width), F32),
        in_specs=[hbm] * 4 + [smem] + [hbm] * 6,
        out_specs=vmem,
        scratch_shapes=[
            pltpu.VMEM((rb, s_local, 2, nz), F32),
            pltpu.VMEM((rb, s_local * width), F32),
            pltpu.VMEM((rb + 2 * (rq + 2), 2 * s_local, zp), BF16),
            pltpu.VMEM(spread.shape, BF16),
            pltpu.VMEM((3, 3, 3, 2, count), BF16),
            pltpu.VMEM((1, count), F32),
            pltpu.VMEM((s_local, n_c, rb, width), BF16),
            pltpu.VMEM((s_local, 2, n_c // 4, 2, rb, width), BF16),
            pltpu.VMEM((s_local, 2, n_c // 4, rb, width), BF16),
            pltpu.VMEM((s_local, n_c // 2, rb, width), BF16),
            pltpu.VMEM((s_local, n_c // 2, rb, width), BF16),
            pltpu.VMEM((3 * SLAB, slices * count), BF16),
            pltpu.VMEM((slices * count, 3 * SLAB), BF16),
            pltpu.VMEM((slices * count, zp), F32),
            pltpu.VMEM((n_e, n_r, rq + 4, 2 * s_local, zp), BF16),
            pltpu.VMEM((2, n_e, n_r, 2, 2 * s_local, zp), BF16),
            pltpu.VMEM((n_e, n_r, rq // band, band, s_local * width), F32),
            pltpu.VMEM((n_q, rq // band, band, s_local * width), F32),
            pltpu.VMEM((n_e, rq + 4, SLAB, zp), F32),
            pltpu.VMEM((n_e, (rq + 4) * SLAB, zp), BF16),
            pltpu.VMEM(k_view.shape, BF16),
            pltpu.VMEM(m_view.shape, BF16),
            pltpu.VMEM(s_view.shape, jnp.int32),
            pltpu.VMEM(fz.shape, BF16),
            pltpu.VMEM(az.shape, BF16),
            pltpu.VMEM(ty.shape, BF16),
            pltpu.VMEM((s_local, ny, 2 * zp), BF16),
            pltpu.VMEM((s_local, ny, 2 * zp), BF16),
            pltpu.VMEM((ny, zp), F32),
            pltpu.VMEM((ny, 2 * zp), BF16),
            pltpu.VMEM((2 * ny, 2 * zp), BF16),
            dma((10,)),
            dma((s_local, n_c)), dma((s_local, n_c)),
            dma((peers,)), dma((peers,)),
            dma((2,)), dma((2, peers)),
            dma((peers,)), dma((peers,)),
            dma((s_local, n_c)), dma((s_local, n_c)),
            dma((s_local, n_c)), dma((s_local, n_c)), dma((s_local, 2)), dma((s_local, 2)),
        ],
        compiler_params=pltpu.CompilerParams(
            collective_id=0, has_side_effects=True, vmem_limit_bytes=GRANT
        ),
        name="cascade",
    )(*operands[:4], dc_weight, *operands[4:])
    return updated.reshape(image.shape)


def solution(mesh):
    return jax.shard_map(
        body,
        mesh=mesh,
        in_specs=(
            P(None, "echo", "coil", "read", None, None),
            P(None, "echo", None),
            P(None, "coil", "read", None, None),
            P("coil", "echo", "read", None, None),
            P(),
            P(),
            P("echo"),
        ),
        out_specs=P("coil", "echo", "read", None, None),
        check_vma=False,
    )
```
